256 devices in a mesh: blk: 128 (over x, z, y), pipe: 2 (over core).
Axes of the slice: x: 4, y: 4, z: 8, core: 2. Of those that a mesh axis runs over, the one named last changes fastest.
Arguments:
- x_saved: bfloat16 [2, 2, 16384, 4096], P('pipe', None, 'blk'), may hold values from -6 to 6
- cotangent: bfloat16 [2, 16384, 4096], P(None, 'blk'), may hold values from -6 to 6
- seq_right: bfloat16 [2, 128, 128, 128], P('pipe', 'blk'), may hold values from -0.5 to 0.5
- seq_left: bfloat16 [2, 128, 128, 128], P('pipe', 'blk'), may hold values from -0.5 to 0.5
- chan_first: bfloat16 [2, 64, 64, 64], P('pipe'), may hold values from -0.75 to 0.75
- chan_second: bfloat16 [2, 64, 64, 64], P('pipe'), may hold values from -0.75 to 0.75
Outputs:
- grad_input: bfloat16 [2, 2, 16384, 4096], P('pipe', None, 'blk')
- grad_right: float32 [2, 128, 128, 128], P('pipe', 'blk')
- grad_left: float32 [2, 128, 128, 128], P('pipe', 'blk')
- grad_first: float32 [2, 64, 64, 64], P('pipe')
- grad_second: float32 [2, 64, 64, 64], P('pipe')
The draws below stay inside these ranges and needn't reach their ends.
All inputs are finite; a program needn't handle non-finite values.
Results may differ from the reference program's by a relative error of at most 0.01.
Values may be sent and summed in bfloat16 or wider, within the bound.
A program may use at most 128 MiB of HBM per device.

```python
import jax
import jax.numpy as jnp
from jax import lax

D = 4096
CB = 64
CNB = 64
SB = 128
NSB = 128
S = 16384
MB = 2
PIPES = 2


def level_of(stream_key, extent, shards, smallest, top_value):
    factor_of = 1.0
    for position, shards_of in shards:
        steps = jax.random.uniform(jax.random.fold_in(jax.random.fold_in(stream_key, 6), position), (shards_of,), jnp.float32, smallest / len(shards), top_value / len(shards))
        factor_of = factor_of * jnp.repeat(jnp.exp(steps), extent[position] // shards_of).reshape((-1,) + (1,) * (len(extent) - 1 - position))
    return factor_of


def centred(own_key, extent, deviation, reach, split=(), dtype=jnp.bfloat16):
    array = deviation * jax.random.normal(own_key, extent, jnp.float32)
    if split:
        array = array * level_of(own_key, extent, split, -0.22, 0.18)
    return jnp.clip(array, -reach, reach).astype(dtype)


def setup_inputs(seed: int = 0) -> dict:
    keys = jax.random.split(jax.random.key(seed), 7)
    x_saved = centred(keys[0], (PIPES, MB, S, D), 1.0, 6.0, ((0, 2), (2, 128)))
    cotangent = centred(keys[1], (MB, S, D), 1.0, 6.0, ((1, 128),))
    seq_right = centred(keys[2], (PIPES, NSB, SB, SB), SB ** -0.5, 0.5, ((0, 2), (1, 128)))
    seq_left = centred(keys[3], (PIPES, SB, NSB, NSB), NSB ** -0.5, 0.5, ((0, 2), (1, 128)))
    chan_first = centred(keys[4], (PIPES, CNB, CB, CB), CB ** -0.5, 0.75, ((0, 2),))
    chan_second = centred(keys[5], (PIPES, CB, CNB, CNB), CNB ** -0.5, 0.75, ((0, 2),))
    return dict(x_saved=x_saved, cotangent=cotangent, seq_right=seq_right, seq_left=seq_left, chan_first=chan_first, chan_second=chan_second)


def rounded(value):
    return lax.optimization_barrier(value.astype(jnp.bfloat16)).astype(jnp.float32)


def layer_backward(activation, grad_out, right_wide, left_wide, first_wide, second_wide):
    act_wide = activation.astype(jnp.float32)
    act_blocks = act_wide.reshape(S, CNB, CB)
    mixed = rounded(jnp.einsum('saj,akj->sak', act_blocks, first_wide))
    hidden = rounded(jnp.einsum('sak,kma->skm', mixed, second_wide))
    hidden_rows = hidden.reshape(NSB, SB, D)
    seq_rows = rounded(jnp.einsum('ikj,ijd->kid', right_wide, hidden_rows))
    carried = jnp.einsum('kmi,kid->kmd', left_wide, seq_rows).reshape(S, D)
    grad_wide = grad_out.astype(jnp.float32)
    gate_grad = rounded(grad_wide * act_wide).reshape(SB, NSB, D)
    left_grad = jnp.einsum('kmd,kid->kmi', gate_grad, seq_rows)
    back_rows = rounded(jnp.einsum('kmi,kmd->ikd', left_wide, gate_grad))
    right_grad = jnp.einsum('ikd,ijd->ikj', back_rows, hidden_rows)
    hidden_grad = rounded(jnp.einsum('ikj,ikd->ijd', right_wide, back_rows)).reshape(S, CB, CNB)
    second_grad = jnp.einsum('skm,sak->kma', hidden_grad, mixed)
    mixed_grad = rounded(jnp.einsum('skm,kma->sak', hidden_grad, second_wide))
    first_grad = jnp.einsum('sak,saj->akj', mixed_grad, act_blocks)
    chan_back = jnp.einsum('sak,akj->saj', mixed_grad, first_wide).reshape(S, D)
    input_grad = (grad_wide * carried + chan_back).astype(jnp.bfloat16)
    return input_grad, right_grad, left_grad, first_grad, second_grad


def reference(x_saved, cotangent, seq_right, seq_left, chan_first, chan_second):
    incoming = [cotangent[micro_index] for micro_index in range(MB)]
    grad_inputs = [None] * PIPES
    grad_rights = [None] * PIPES
    grad_lefts = [None] * PIPES
    grad_firsts = [None] * PIPES
    grad_seconds = [None] * PIPES
    for section in range(PIPES - 1, -1, -1):
        right_wide = seq_right[section].astype(jnp.float32)
        left_wide = seq_left[section].astype(jnp.float32)
        first_wide = chan_first[section].astype(jnp.float32)
        second_wide = chan_second[section].astype(jnp.float32)
        right_acc = jnp.zeros((NSB, SB, SB), jnp.float32)
        left_acc = jnp.zeros((SB, NSB, NSB), jnp.float32)
        first_acc = jnp.zeros((CNB, CB, CB), jnp.float32)
        second_acc = jnp.zeros((CB, CNB, CNB), jnp.float32)
        produced = []
        for micro_index in range(MB):
            result = layer_backward(x_saved[section, micro_index], incoming[micro_index],
                                    right_wide, left_wide, first_wide, second_wide)
            produced.append(result[0])
            right_acc = right_acc + result[1]
            left_acc = left_acc + result[2]
            first_acc = first_acc + result[3]
            second_acc = second_acc + result[4]
        incoming = produced
        grad_inputs[section] = jnp.stack(produced)
        grad_rights[section] = right_acc
        grad_lefts[section] = left_acc
        grad_firsts[section] = first_acc
        grad_seconds[section] = second_acc
    return (jnp.stack(grad_inputs), jnp.stack(grad_rights), jnp.stack(grad_lefts),
            jnp.stack(grad_firsts), jnp.stack(grad_seconds))
```

```python
import functools

import jax
import jax.numpy as jnp
from jax import lax
from jax.experimental import pallas as pl
from jax.experimental.pallas import tpu as pltpu
from jax.sharding import PartitionSpec as P

MESH = pl.DeviceIdType.MESH
NX, NZ, NY = 4, 8, 4
NB = NX * NZ * NY


def full_barrier(me):
    barrier = pltpu.get_barrier_semaphore()

    def greet(step, carry):
        peer = lax.rem(me + step, NB)
        pl.semaphore_signal(barrier, inc=1, device_id={"blk": peer}, device_id_type=MESH)
        return carry

    lax.fori_loop(1, NB, greet, 0)
    pl.semaphore_wait(barrier, NB - 1)


def exchange_kernel(count, *refs):
    sources, targets = refs[:count], refs[count : 2 * count]
    send_sem, recv_sem, own_sem = refs[2 * count :]
    me = lax.axis_index("blk")
    full_barrier(me)
    for index in range(count):
        src, dst = sources[index], targets[index]

        def send(step, carry):
            peer = lax.rem(me + step, NB)
            pltpu.make_async_remote_copy(
                src_ref=src.at[peer],
                dst_ref=dst.at[me],
                send_sem=send_sem.at[index],
                recv_sem=recv_sem.at[index],
                device_id={"blk": peer},
                device_id_type=MESH,
            ).start()
            return carry

        lax.fori_loop(1, NB, send, 0)
        own = pltpu.make_async_copy(src.at[me], dst.at[me], own_sem)
        own.start()
        own.wait()
    for index in range(count):
        src, dst = sources[index], targets[index]
        rest = pl.ds(0, NB - 1)
        pltpu.make_async_copy(src.at[rest], dst.at[rest], send_sem.at[index]).wait()
        pltpu.make_async_copy(src.at[rest], dst.at[rest], recv_sem.at[index]).wait()


def exchange(blocks, ident):
    count = len(blocks)
    width = blocks[0].shape[-1]
    shaped = [b.reshape(NB, width // 128, 128) for b in blocks]
    outs = pl.pallas_call(
        functools.partial(exchange_kernel, count),
        name=f"exchange_{ident}",
        out_shape=[jax.ShapeDtypeStruct(s.shape, s.dtype) for s in shaped],
        in_specs=[pl.BlockSpec(memory_space=pltpu.VMEM)] * count,
        out_specs=[pl.BlockSpec(memory_space=pltpu.VMEM)] * count,
        scratch_shapes=[
            pltpu.SemaphoreType.DMA((count,)),
            pltpu.SemaphoreType.DMA((count,)),
            pltpu.SemaphoreType.DMA,
        ],
        compiler_params=pltpu.CompilerParams(
            collective_id=ident, has_side_effects=True, vmem_limit_bytes=32 << 20
        ),
    )(*shaped)
    return [o.reshape(NB, width) for o in outs]


def reduce_kernel(a_ref, o_ref, sx, rx, ax, sy, ry, ay, sz, rz, gz, gy, gx, send_sem, recv_sem):
    me = lax.axis_index("blk")
    x, z, y = lax.div(me, NZ * NY), lax.rem(lax.div(me, NY), NZ), lax.rem(me, NY)

    def at(px, pz, py):
        return {"blk": (px * NZ + pz) * NY + py}

    peers = []
    for d in range(1, NX):
        peers.append((at(lax.rem(x + d, NX), z, y), at(lax.rem(x + NX - d, NX), z, y)))
    for d in range(1, NY):
        peers.append((at(x, z, lax.rem(y + d, NY)), at(x, z, lax.rem(y + NY - d, NY))))
    for d in range(1, NZ):
        peers.append((at(x, lax.rem(z + d, NZ), y), at(x, lax.rem(z + NZ - d, NZ), y)))
    barrier = pltpu.get_barrier_semaphore()
    for to, _ in peers:
        pl.semaphore_signal(barrier, inc=1, device_id=to, device_id_type=MESH)
    pl.semaphore_wait(barrier, len(peers))

    slot = [0]

    def scatter(values, coord, size, stage, landing, base):
        rows = landing.shape[1]
        copies = []
        for d in range(1, size):
            owner = lax.rem(coord + d, size)
            copy = pltpu.make_async_remote_copy(
                src_ref=stage.at[pl.ds(pl.multiple_of(owner * rows, rows), rows)],
                dst_ref=landing.at[d],
                send_sem=send_sem.at[base + d],
                recv_sem=recv_sem.at[base + d],
                device_id=peers[base + d - 1][0],
                device_id_type=MESH,
            )
            copy.start()
            copies.append(copy)
        for copy in copies:
            copy.wait()
        total = values[pl.ds(pl.multiple_of(coord * rows, rows), rows), :]
        for d in range(1, size):
            total = total + landing[d].astype(jnp.float32)
        return total

    def gather(coord, size, src, landing, base, sem_base):
        copies = []
        for d in range(1, size):
            copy = pltpu.make_async_remote_copy(
                src_ref=src,
                dst_ref=landing.at[coord],
                send_sem=send_sem.at[sem_base + d],
                recv_sem=recv_sem.at[sem_base + d],
                device_id=peers[base + d - 1][0],
                device_id_type=MESH,
            )
            copy.start()
            copies.append(copy)
        for copy in copies:
            copy.wait()

    sx[...] = a_ref[...].astype(jnp.bfloat16)
    ax[...] = scatter(a_ref, x, NX, sx, rx, 0)
    sy[...] = ax[...].astype(jnp.bfloat16)
    ay[...] = scatter(ax, y, NY, sy, ry, NX - 1)
    sz[...] = ay[...].astype(jnp.bfloat16)
    zb = NX + NY - 2
    result = scatter(ay, z, NZ, sz, rz, zb).astype(jnp.bfloat16)
    gz[z] = result
    count = NX + NY + NZ - 3
    gather(z, NZ, gz.at[z], gz, zb, count + zb)
    mid = gz[...]
    gy[y] = mid
    gather(y, NY, gy.at[y], gy, NX - 1, count + NX - 1)
    gx[x] = gy[...]
    gather(x, NX, gx.at[x], gx, 0, count)
    o_ref[...] = gx[...].astype(jnp.float32).reshape(o_ref.shape)


def reduce_all(values, ident):
    rows = values.shape[0]
    rx, ry, rz = rows // NX, rows // NX // NY, rows // NB
    f32, bf16 = jnp.float32, jnp.bfloat16
    n_sem = 2 * (NX + NY + NZ - 3) + 1
    return pl.pallas_call(
        reduce_kernel,
        name=f"reduce_{ident}",
        out_shape=jax.ShapeDtypeStruct(values.shape, f32),
        in_specs=[pl.BlockSpec(memory_space=pltpu.VMEM)],
        out_specs=pl.BlockSpec(memory_space=pltpu.VMEM),
        scratch_shapes=[
            pltpu.VMEM((rows, 128), bf16),
            pltpu.VMEM((NX, rx, 128), bf16),
            pltpu.VMEM((rx, 128), f32),
            pltpu.VMEM((rx, 128), bf16),
            pltpu.VMEM((NY, ry, 128), bf16),
            pltpu.VMEM((ry, 128), f32),
            pltpu.VMEM((ry, 128), bf16),
            pltpu.VMEM((NZ, rz, 128), bf16),
            pltpu.VMEM((NZ, rz, 128), bf16),
            pltpu.VMEM((NY, NZ, rz, 128), bf16),
            pltpu.VMEM((NX, NY, NZ, rz, 128), bf16),
            pltpu.SemaphoreType.DMA((n_sem,)),
            pltpu.SemaphoreType.DMA((n_sem,)),
        ],
        compiler_params=pltpu.CompilerParams(
            collective_id=ident, has_side_effects=True, vmem_limit_bytes=40 << 20
        ),
    )(values)


def dot(spec, a, b):
    return jnp.einsum(spec, a, b, preferred_element_type=jnp.float32)


def forward(act, right, first, second):
    bf16 = jnp.bfloat16
    width = act.shape[1]
    cols = act.T.reshape(first.shape[0], first.shape[2], act.shape[0])
    mixed = dot("akj,ajs->aks", first, cols).astype(bf16)
    mixed_k = jnp.transpose(mixed, (1, 0, 2))
    hidden = dot("kma,kas->kms", second, mixed_k).astype(bf16).reshape(width, -1)
    rows = dot("kj,dj->kd", right, hidden).astype(bf16)
    return cols, mixed_k, hidden, rows


def gate(act, grad_out, left):
    f32, bf16 = jnp.float32, jnp.bfloat16
    gate_grad = (grad_out.astype(f32) * act.astype(f32)).astype(bf16)
    back = dot("mi,md->id", left, gate_grad).astype(bf16)
    return gate_grad, back


def finish(gate_grad, grad_out, gathered, returned, cols, mixed_k, hidden, weights):
    right, left, first, second = weights
    f32, bf16 = jnp.float32, jnp.bfloat16
    tokens, width = grad_out.shape
    carried = dot("mi,id->md", left, gathered)
    left_grad = dot("md,id->mi", gate_grad, gathered)
    right_grad = dot("kd,dj->kj", returned, hidden)
    hidden_grad = dot("kj,kd->dj", right, returned).astype(bf16)
    hidden_grad = hidden_grad.reshape(second.shape[0], second.shape[1], tokens)
    second_grad = dot("kms,kas->kma", hidden_grad, mixed_k)
    mixed_grad = dot("kma,kms->kas", second, hidden_grad).astype(bf16)
    mixed_grad = jnp.transpose(mixed_grad, (1, 0, 2))
    first_grad = dot("aks,ajs->akj", mixed_grad, cols)
    chan_back = dot("akj,aks->ajs", first, mixed_grad).reshape(width, tokens).T
    input_grad = (grad_out.astype(f32) * carried + chan_back).astype(bf16)
    return input_grad, right_grad, left_grad, first_grad, second_grad


def body(x_saved, cotangent, seq_right, seq_left, chan_first, chan_second):
    core = lax.axis_index("pipe")
    low = core == 0

    def swap(value):
        return lax.ppermute(value, "pipe", [(0, 1), (1, 0)])

    def pick(pair, index):
        return lax.dynamic_index_in_dim(pair, index, 0, keepdims=False)

    saved = x_saved[0]
    mine = (pick(saved, core), seq_right[0, 0], seq_left[0, 0], chan_first[0], chan_second[0])
    theirs = tuple(
        swap(v) for v in (pick(saved, 1 - core), seq_right[0, 0], seq_left[0, 0], chan_first[0], chan_second[0])
    )
    upper = [jnp.where(low, t, m) for m, t in zip(mine, theirs)]
    lower = [jnp.where(low, m, t) for m, t in zip(mine, theirs)]
    grad_out = pick(cotangent, core)

    act1, w1 = upper[0], upper[1:]
    act0, w0 = lower[0], lower[1:]
    cols1, mixed1, hidden1, rows1 = forward(act1, w1[0], w1[2], w1[3])
    gate1, back1 = gate(act1, grad_out, w1[1])
    cols0, mixed0, hidden0, rows0 = forward(act0, w0[0], w0[2], w0[3])
    gathered1, returned1, gathered0 = exchange([rows1, back1, rows0], 1)
    res1 = finish(gate1, grad_out, gathered1, returned1, cols1, mixed1, hidden1, w1)
    grad_mid = res1[0]
    gate0, back0 = gate(act0, grad_mid, w0[1])
    (returned0,) = exchange([back0], 2)
    res0 = finish(gate0, grad_mid, gathered0, returned0, cols0, mixed0, hidden0, w0)

    own = [jnp.where(low, b, a) for a, b in zip(res1, res0)]
    other = [swap(jnp.where(low, a, b)) for a, b in zip(res1, res0)]
    grad_input = jnp.stack([jnp.where(low, own[0], other[0]), jnp.where(low, other[0], own[0])])
    right_grad, left_grad, first_grad, second_grad = [a + b for a, b in zip(own[1:], other[1:])]
    flat = jnp.concatenate([first_grad.reshape(-1, 128), second_grad.reshape(-1, 128)])
    total = reduce_all(flat, 3)
    half = flat.shape[0] // 2
    first_total = total[:half].reshape(first_grad.shape)
    second_total = total[half:].reshape(second_grad.shape)
    return (
        grad_input[None],
        right_grad[None, None],
        left_grad[None, None],
        first_total[None],
        second_total[None],
    )


def solution(mesh):
    in_specs = (
        P("pipe", None, "blk", None),
        P(None, "blk", None),
        P("pipe", "blk", None, None),
        P("pipe", "blk", None, None),
        P("pipe", None, None, None),
        P("pipe", None, None, None),
    )
    out_specs = (
        P("pipe", None, "blk", None),
        P("pipe", "blk", None, None),
        P("pipe", "blk", None, None),
        P("pipe", None, None, None),
        P("pipe", None, None, None),
    )
    return jax.shard_map(body, mesh=mesh, in_specs=in_specs, out_specs=out_specs, check_vma=False)
```

```python
import jax
import jax.numpy as jnp
from jax import lax
from jax.experimental import pallas as pl
from jax.experimental.pallas import tpu as pltpu
from jax.sharding import PartitionSpec as P

MESH = pl.DeviceIdType.MESH
F32, BF16 = jnp.float32, jnp.bfloat16
NX, NZ, NY = 4, 8, 4
NB = NX * NZ * NY
T = 128
D = 4096
HALF = D // 2
NK = 64
TILE = 512
HR = 2048


def mm(a, b, ca=1, cb=0):
    return lax.dot_general(a, b, (((ca,), (cb,)), ((), ())), preferred_element_type=F32)


def aligned(index, size):
    return pl.ds(pl.multiple_of(index * size, size), size)


def kernel(
    x_in, cot_in, right_in, left_in, first_in, second_in,
    gi_out, right_out, left_out, chan_out,
    x_buf, right_buf, left_buf, first_buf, second_buf,
    gy_buf, gi_buf, gate_buf, pair_buf, mt_buf, mk_buf, ht_buf, hg_buf, cb_buf,
    rexp, lexp, lexp_t,
    send_f, recv_f, send_b, recv_b, dummy, acc, tmp,
    grads, sib, stage1, land1, acc1, stage2, land2, acc2, stage3, land3, gz, gy2, gx, swap_buf,
    lr, lr_sib,
    in_sem, ex_sem, cot_sem, a2a_send, a2a_recv, red_send, red_recv,
    gi_loc, gi_send, gi_recv, lr_send, lr_recv, swap_send, swap_recv, out_sem,
):
    me = lax.axis_index("blk")
    core = lax.axis_index("pipe")
    other = 1 - core
    sibling = {"pipe": other}
    px, pz, py = lax.div(me, NZ * NY), lax.rem(lax.div(me, NY), NZ), lax.rem(me, NY)

    local = (
        (x_in.at[core], x_buf), (left_in, left_buf), (right_in, right_buf),
        (first_in, first_buf), (second_in, second_buf),
    )
    for i, (src, dst) in enumerate(local):
        pltpu.make_async_copy(src, dst.at[core], in_sem.at[core, i]).start()
    cot_copy = pltpu.make_async_copy(cot_in.at[core], gy_buf, cot_sem)
    cot_copy.start()

    barrier = pltpu.get_barrier_semaphore()

    def greet(step, carry):
        peer = lax.rem(me + step, NB)
        pl.semaphore_signal(barrier, inc=1, device_id={"blk": peer}, device_id_type=MESH)
        return carry

    pl.semaphore_signal(barrier, inc=1, device_id=sibling, device_id_type=MESH)
    lax.fori_loop(1, NB, greet, 0)
    pl.semaphore_wait(barrier, NB)

    remote = (
        (x_in.at[other], x_buf), (left_in, left_buf), (right_in, right_buf),
        (first_in, first_buf), (second_in, second_buf),
    )
    ex_copies = []
    for i, (src, dst) in enumerate(remote):
        copy = pltpu.make_async_remote_copy(
            src_ref=src, dst_ref=dst.at[core], send_sem=ex_sem.at[i], recv_sem=in_sem.at[core, i],
            device_id=sibling, device_id_type=MESH,
        )
        copy.start()
        ex_copies.append(copy)

    def await_input(section, i):
        ref = (x_buf, left_buf, right_buf, first_buf, second_buf)[i].at[section]
        pltpu.make_async_copy(ref, ref, in_sem.at[section, i]).wait()

    def all_to_all(src, dst, ident, lo, size):
        columns = pl.ds(lo, size)

        def rows(i):
            return pl.ds(pl.multiple_of(2 * i, 2), 2)

        def send(step, carry):
            peer = lax.rem(me + step, NB)
            pltpu.make_async_remote_copy(
                src_ref=src.at[rows(peer), columns], dst_ref=dst.at[rows(me), columns],
                send_sem=a2a_send.at[ident], recv_sem=a2a_recv.at[ident],
                device_id={"blk": peer}, device_id_type=MESH,
            ).start()
            return carry

        lax.fori_loop(1, NB, send, 0)
        pltpu.make_async_copy(
            src.at[rows(me), columns], dst.at[rows(me), columns], a2a_recv.at[ident]
        ).start()
        pltpu.make_async_copy(
            src.at[rows(me), columns], dummy.at[ident, :, columns], a2a_send.at[ident]
        ).start()

    def await_block(ref, sem, ident, lo, size):
        part = ref.at[:, pl.ds(lo, size)]
        pltpu.make_async_copy(part, part, sem.at[ident]).wait()

    def expand(section):
        row = lax.broadcasted_iota(jnp.int32, (2 * T, T), 0)
        col = lax.broadcasted_iota(jnp.int32, (2 * T, T), 1)
        left = left_buf[section]
        for h in range(2):
            spread = (row == 2 * col + h).astype(F32).astype(BF16)
            part = slice(h * T, (h + 1) * T)
            lexp[section, part, :] = mm(left, spread, 1, 1).astype(BF16)
            lexp_t[section, :, part] = mm(spread, left, 1, 1).astype(BF16)

    def expand_right(section):
        row = lax.broadcasted_iota(jnp.int32, (2 * T, T), 0)
        col = lax.broadcasted_iota(jnp.int32, (2 * T, T), 1)
        right = right_buf[section]
        for h in range(2):
            spread = (row == 2 * col + h).astype(F32).astype(BF16)
            part = slice(h * T, (h + 1) * T)
            rexp[section, :, part] = mm(spread, right).astype(BF16)

    def build_pairs(section):
        row = lax.broadcasted_iota(jnp.int32, (NK, T), 0)
        col = lax.broadcasted_iota(jnp.int32, (NK, T), 1)
        twice = ((col == row) | (col == row + NK)).astype(F32).astype(BF16)
        low = lax.broadcasted_iota(jnp.int32, (T, T), 0) < NK
        first_half = lax.broadcasted_iota(jnp.int32, (T, T), 1) < NK

        def step(b, carry):
            rows = aligned(b, T)
            both = mm(first_buf[section, rows, :], twice)
            pair_buf[section, rows, :] = jnp.where(low == first_half, both, 0.0).astype(BF16)
            return carry

        lax.fori_loop(0, NK // 2, step, 0, unroll=4)

    def gate(section, grad_out, sent):
        def step(i, carry):
            cs = aligned(i, TILE)
            for h in range(2):
                wide = pl.ds(pl.multiple_of(i * TILE + h * HALF, TILE), TILE)
                value = grad_out[:, wide].astype(F32) * x_buf[section, :, wide].astype(F32)
                gate_buf[h * T : (h + 1) * T, cs] = value.astype(BF16)
            sent[:, cs] = mm(lexp_t[section], gate_buf[:, cs]).astype(BF16)
            return carry

        lax.fori_loop(0, HALF // TILE, step, 0)

    def swap_blocks(src, dst):
        def step(g, carry):
            block = src[:, pl.ds(pl.multiple_of(g * 16, 16), 16), :]
            dst[aligned(g, 16), :, :] = jnp.swapaxes(block, 0, 1)
            return carry

        lax.fori_loop(0, NK // 16, step, 0)

    def forward(section, sent):
        def mixed(b, carry):
            cols = aligned(b, T)
            out = mm(pair_buf[section, cols, :], x_buf[section, :, cols], 1, 1)
            mt_buf[aligned(b, 2)] = out.astype(BF16).reshape(2, NK, T)
            return carry

        lax.fori_loop(0, NK // 2, mixed, 0, unroll=4)
        swap_blocks(mt_buf, mk_buf.at[section])

        def hidden(k, carry):
            rows = aligned(k, NK)
            for h in range(2):
                kk = k + h * (NK // 2)
                out = mm(second_buf[section, kk], mk_buf[section, kk])
                ht_buf[section, rows, h * T : (h + 1) * T] = out.astype(BF16)
            return carry

        lax.fori_loop(0, NK // 2, hidden, 0, unroll=4)

        def rows_of(i, carry):
            cs = aligned(i, TILE)
            sent[:, cs] = mm(rexp[section], ht_buf[section, cs, :], 1, 1).astype(BF16)
            return carry

        lax.fori_loop(0, HALF // TILE, rows_of, 0)

    def fold(target):
        even = lax.rem(lax.broadcasted_iota(jnp.int32, (2 * T, T), 0), 2) == 0
        tmp[...] = jnp.where(even, acc[:, :T], acc[:, T:])
        target[...] = tmp[pl.ds(0, T, stride=2), :] + tmp[pl.ds(1, T, stride=2), :]

    def channel_back(section, returned):
        acc[...] = jnp.zeros_like(acc)

        def step(i, carry):
            cs = aligned(i, TILE)
            acc[...] += mm(returned[:, cs], ht_buf[section, cs, :])
            hg_buf[cs, :] = mm(returned[:, cs], rexp[section], 0, 0).astype(BF16)
            return carry

        lax.fori_loop(0, HALF // TILE, step, 0)
        fold(lr.at[section, 0])
        first_half = lax.broadcasted_iota(jnp.int32, (NK, T), 1) < NK

        def pair(b, carry):
            for h in range(2):
                k0 = 2 * b + h * (NK // 2)
                grad = hg_buf[aligned(b, T), h * T : (h + 1) * T]
                mix = mk_buf[section, pl.ds(k0, 2)].reshape(T, T)
                outer = mm(grad, mix, 1, 1)
                grads[section, 1, pl.ds(pl.multiple_of(k0 * (NK // 2), NK), NK), :] = jnp.where(
                    first_half, outer[:NK], outer[NK:]
                )
                for q in range(2):
                    back = mm(second_buf[section, k0 + q], grad[q * NK : (q + 1) * NK], 0, 0)
                    mt_buf[k0 + q] = back.astype(BF16)
            return carry

        lax.fori_loop(0, NK // 4, pair, 0, unroll=2)
        swap_blocks(mt_buf, mg_view)

        def columns(b, carry):
            cols = aligned(b, T)
            mixed_grad = mg_view[aligned(b, 2)].reshape(T, T)
            outer = mm(mixed_grad, x_buf[section, :, cols])
            grads[section, 0, aligned(b, NK), :] = jnp.where(first_half, outer[:NK], outer[NK:])
            cb_buf[:, cols] = mm(mixed_grad, pair_buf[section, cols, :], 0, 0)
            return carry

        lax.fori_loop(0, NK // 2, columns, 0, unroll=4)

    mg_view = mk_buf.at[2]

    def carry_out(section, gathered, grad_out, lo, size):
        def step(i, carry):
            off = lo + i * TILE
            cs = pl.ds(pl.multiple_of(off, TILE), TILE)
            block = gathered[:, cs]
            carried = mm(lexp[section], block)
            for h in range(2):
                wide = pl.ds(pl.multiple_of(off + h * HALF, TILE), TILE)
                value = grad_out[:, wide].astype(F32) * carried[h * T : (h + 1) * T] + cb_buf[:, wide]
                gi_buf[section, :, wide] = value.astype(BF16)
            acc[...] += mm(block, gate_buf[:, cs], 1, 1)
            return carry

        lax.fori_loop(0, size // TILE, step, 0)

    def finish_left(section):
        fold(tmp2)
        lr[section, 1] = tmp2[...].T

    tmp2 = acc2.at[2]

    def send_input_grad(section):
        @pl.when(core == section)
        def _():
            pltpu.make_async_copy(gi_buf.at[section], gi_out.at[core], gi_loc).start()

        @pl.when(core != section)
        def _():
            pltpu.make_async_remote_copy(
                src_ref=gi_buf.at[section], dst_ref=gi_out.at[core], send_sem=gi_send, recv_sem=gi_recv,
                device_id=sibling, device_id_type=MESH,
            ).start()

    is_low = core == 0
    coord1, coord2 = jnp.where(is_low, px, py), jnp.where(is_low, py, px)
    stride1, stride2 = jnp.where(is_low, NZ * NY, 1), jnp.where(is_low, 1, NZ * NY)
    axes = ((coord1, stride1, NX), (coord2, stride2, NY), (pz, NY, NZ))

    def hop(axis, d):
        coord, stride, size = axes[axis]
        return {"blk": me + (lax.rem(coord + d, size) - coord) * stride}

    def copies(section, base, axis, src_of, dst_of):
        size = axes[axis][2]
        return [
            pltpu.make_async_remote_copy(
                src_ref=src_of(d), dst_ref=dst_of(d),
                send_sem=red_send.at[section, base + d], recv_sem=red_recv.at[section, base + d],
                device_id=hop(axis, d), device_id_type=MESH,
            )
            for d in range(1, size)
        ]

    def scatter(section, base, axis, stage, landing):
        coord, _, size = axes[axis]
        rows = landing.shape[2]
        return copies(
            section, base, axis,
            lambda d: stage.at[section, aligned(lax.rem(coord + d, size), rows)],
            lambda d: landing.at[section, d],
        )

    def gather(section, base, axis, buf):
        coord = axes[axis][0]
        return copies(
            section, base, axis,
            lambda d: buf.at[section, coord],
            lambda d: buf.at[section, coord],
        )

    def sib_copy(section):
        return pltpu.make_async_remote_copy(
            src_ref=grads.at[section, other], dst_ref=sib.at[section],
            send_sem=red_send.at[section, 0], recv_sem=red_recv.at[section, 0],
            device_id=sibling, device_id_type=MESH,
        )

    def start(group):
        for c in group:
            c.start()

    def finish(group):
        for c in group:
            c.wait()

    def reduce_stage(section, number):
        def s1():
            return scatter(section, 0, 0, stage1, land1)

        def s2():
            return scatter(section, 3, 1, stage2, land2)

        def s3():
            return scatter(section, 6, 2, stage3, land3)

        def g3():
            return gather(section, 13, 2, gz)

        def g2():
            return gather(section, 20, 1, gy2)

        def g1():
            return gather(section, 23, 0, gx)

        def settle(values, coord, landing, size):
            rows = landing.shape[2]
            total = values[aligned(coord, rows), :]
            for d in range(1, size):
                total = total + landing[section, d].astype(F32)
            return total

        if number == 0:
            sib_copy(section).start()
        elif number == 1:
            sib_copy(section).wait()
            mine = grads.at[section, core]

            def add(i, carry):
                rows = aligned(i, 256)
                total = mine[rows, :] + sib[section, rows, :]
                sib[section, rows, :] = total
                stage1[section, rows, :] = total.astype(BF16)
                return carry

            lax.fori_loop(0, HR // 256, add, 0)
            start(s1())
        elif number == 2:
            finish(s1())
            value = settle(sib.at[section], coord1, land1, NX)
            acc1[section] = value
            stage2[section] = value.astype(BF16)
            start(s2())
        elif number == 3:
            finish(s2())
            value = settle(acc1.at[section], coord2, land2, NY)
            acc2[section] = value
            stage3[section] = value.astype(BF16)
            start(s3())
        elif number == 4:
            finish(s3())
            value = settle(acc2.at[section], pz, land3, NZ)
            gz[section, pz] = value.astype(BF16)
            start(g3())
        elif number == 5:
            finish(g3())
            gy2[section, coord2] = gz[section].reshape(T, T)
            start(g2())
        elif number == 6:
            finish(g2())
            gx[section, coord1] = gy2[section].reshape(NY * T, T)
            start(g1())
        else:
            finish(g1())

    cot_copy.wait()
    await_input(1, 1)
    expand(1)
    await_input(1, 0)
    gate(1, gy_buf, send_b.at[1])
    all_to_all(send_b.at[1], recv_b.at[1], 0, 0, HALF)

    await_input(1, 2)
    expand_right(1)
    await_input(1, 3)
    build_pairs(1)
    await_input(1, 4)
    forward(1, send_f.at[1])
    all_to_all(send_f.at[1], recv_f.at[1], 1, 0, HALF)

    for i in range(5):
        await_input(0, i)
    expand(0)
    expand_right(0)
    build_pairs(0)
    forward(0, send_f.at[0])
    all_to_all(send_f.at[0], recv_f.at[0], 2, 0, HALF // 2)

    await_block(recv_b.at[1], a2a_recv, 0, 0, HALF)
    channel_back(1, recv_b.at[1])
    reduce_stage(1, 0)
    reduce_stage(1, 1)

    await_block(recv_f.at[1], a2a_recv, 1, 0, HALF)
    acc[...] = jnp.zeros_like(acc)
    carry_out(1, recv_f.at[1], gy_buf, 0, HALF)
    finish_left(1)
    gate(0, gi_buf.at[1], send_b.at[0])
    all_to_all(send_b.at[0], recv_b.at[0], 3, 0, HALF)
    all_to_all(send_f.at[0], recv_f.at[0], 4, HALF // 2, HALF // 2)
    send_input_grad(1)
    for number in range(2, 8):
        reduce_stage(1, number)

    await_block(recv_b.at[0], a2a_recv, 3, 0, HALF)
    channel_back(0, recv_b.at[0])
    reduce_stage(0, 0)
    reduce_stage(0, 1)
    await_block(recv_f.at[0], a2a_recv, 2, 0, HALF // 2)
    acc[...] = jnp.zeros_like(acc)
    carry_out(0, recv_f.at[0], gi_buf.at[1], 0, HALF // 2)
    reduce_stage(0, 2)
    await_block(recv_f.at[0], a2a_recv, 4, HALF // 2, HALF // 2)
    carry_out(0, recv_f.at[0], gi_buf.at[1], HALF // 2, HALF // 2)
    send_input_grad(0)
    finish_left(0)
    lr_copy = pltpu.make_async_remote_copy(
        src_ref=lr.at[other], dst_ref=lr_sib, send_sem=lr_send, recv_sem=lr_recv,
        device_id=sibling, device_id_type=MESH,
    )
    lr_copy.start()
    for number in range(3, 8):
        reduce_stage(0, number)
    swap_copy = pltpu.make_async_remote_copy(
        src_ref=gx.at[other], dst_ref=swap_buf, send_sem=swap_send, recv_sem=swap_recv,
        device_id=sibling, device_id_type=MESH,
    )
    swap_copy.start()
    chan_out[core] = gx[core].reshape(HR, T).astype(F32)
    lr_copy.wait()
    right_out[...] = lr[core, 0] + lr_sib[0]
    left_out[...] = lr[core, 1] + lr_sib[1]
    swap_copy.wait()
    chan_out[other] = swap_buf[...].reshape(HR, T).astype(F32)

    for copy in ex_copies:
        copy.wait_send()
    await_block(send_b.at[1], a2a_send, 0, 0, HALF)
    await_block(send_f.at[1], a2a_send, 1, 0, HALF)
    await_block(send_f.at[0], a2a_send, 2, 0, HALF // 2)
    await_block(send_b.at[0], a2a_send, 3, 0, HALF)
    await_block(send_f.at[0], a2a_send, 4, HALF // 2, HALF // 2)
    pltpu.make_async_copy(gi_buf.at[0], gi_out.at[0], gi_loc).wait()
    pltpu.make_async_copy(gi_buf.at[0], gi_out.at[0], gi_send).wait()
    pltpu.make_async_copy(gi_buf.at[0], gi_out.at[0], gi_recv).wait()


def body(x_saved, cotangent, seq_right, seq_left, chan_first, chan_second):
    v, dma = pltpu.VMEM, pltpu.SemaphoreType.DMA
    anywhere = pl.BlockSpec(memory_space=pl.ANY)
    vmem = pl.BlockSpec(memory_space=pltpu.VMEM)
    gi, right, left, chan = pl.pallas_call(
        kernel,
        name="monarch_backward",
        out_shape=[
            jax.ShapeDtypeStruct((2, T, D), BF16),
            jax.ShapeDtypeStruct((T, T), F32),
            jax.ShapeDtypeStruct((T, T), F32),
            jax.ShapeDtypeStruct((2, HR, T), F32),
        ],
        in_specs=[anywhere] * 6,
        out_specs=[anywhere, vmem, vmem, vmem],
        scratch_shapes=[
            v((2, T, D), BF16), v((2, T, T), BF16), v((2, T, T), BF16),
            v((2, D, NK), BF16), v((2, NK, NK, NK), BF16),
            v((T, D), BF16), v((2, T, D), BF16), v((2 * T, HALF), BF16), v((2, D, T), BF16),
            v((NK, NK, T), BF16), v((3, NK, NK, T), BF16), v((2, HALF, 2 * T), BF16),
            v((HALF, 2 * T), BF16), v((T, D), F32),
            v((2, 2 * T, 2 * T), BF16), v((2, 2 * T, 2 * T), BF16), v((2, 2 * T, 2 * T), BF16),
            v((2, 2 * T, HALF), BF16), v((2, 2 * T, HALF), BF16),
            v((2, 2 * T, HALF), BF16), v((2, 2 * T, HALF), BF16),
            v((5, 2, HALF), BF16), v((2 * T, 2 * T), F32), v((2 * T, T), F32),
            v((2, 2, HR, T), F32), v((2, HR, T), F32),
            v((2, HR, T), BF16), v((2, NX, HR // NX, T), BF16), v((2, HR // NX, T), F32),
            v((2, HR // NX, T), BF16), v((2, NY, T, T), BF16), v((3, T, T), F32),
            v((2, T, T), BF16), v((2, NZ, T // NZ, T), BF16),
            v((2, NZ, T // NZ, T), BF16), v((2, NY, T, T), BF16), v((2, NX, NY * T, T), BF16),
            v((NX, NY * T, T), BF16),
            v((2, 2, T, T), F32), v((2, T, T), F32),
            dma((2, 5)), dma((5,)), dma, dma((5,)), dma((5,)), dma((2, 27)), dma((2, 27)),
            dma, dma, dma, dma, dma, dma, dma, dma,
        ],
        compiler_params=pltpu.CompilerParams(
            collective_id=1, has_side_effects=True, vmem_limit_bytes=64_000_000
        ),
    )(
        x_saved[0], cotangent, seq_right[0, 0], seq_left[0, 0],
        chan_first[0].reshape(D, NK), chan_second[0],
    )

    def unpack(packed):
        return packed.reshape(NK // 2, NK, 2, NK).transpose(0, 2, 1, 3).reshape(1, NK, NK, NK)

    return (gi[None], right[None, None], left[None, None], unpack(chan[0]), unpack(chan[1]))


def solution(mesh):
    in_specs = (
        P("pipe", None, "blk", None),
        P(None, "blk", None),
        P("pipe", "blk", None, None),
        P("pipe", "blk", None, None),
        P("pipe", None, None, None),
        P("pipe", None, None, None),
    )
    out_specs = (
        P("pipe", None, "blk", None),
        P("pipe", "blk", None, None),
        P("pipe", "blk", None, None),
        P("pipe", None, None, None),
        P("pipe", None, None, None),
    )
    return jax.shard_map(body, mesh=mesh, in_specs=in_specs, out_specs=out_specs, check_vma=False)
```

```python
import jax
import jax.numpy as jnp
from jax import lax
from jax.experimental import pallas as pl
from jax.experimental.pallas import tpu as pltpu
from jax.sharding import PartitionSpec as P

MESH = pl.DeviceIdType.MESH
F32, BF16 = jnp.float32, jnp.bfloat16
NX, NZ, NY = 4, 8, 4
NB = NX * NZ * NY
T = 128
D = 4096
HALF = D // 2
NK = 64
TILE = 512
HR = 2048


def mm(a, b, ca=1, cb=0):
    return lax.dot_general(a, b, (((ca,), (cb,)), ((), ())), preferred_element_type=F32)


def aligned(index, size):
    return pl.ds(pl.multiple_of(index * size, size), size)


def kernel(
    x_in, cot_in, right_in, left_in, first_in, second_in,
    gi_out, right_out, left_out, first_out, second_out,
    x_buf, right_buf, left_buf, first_buf, second_buf,
    gy_buf, gi_buf, gate_buf, pair_buf, mt_buf, mk_buf, ht_buf, hg_buf, cb_buf,
    rexp, lexp, lexp_t,
    send_f, recv_f, send_b, recv_b, dummy, acc, tmp,
    grads, sib, stage1, land1, acc1, stage2, land2, acc2, stage3, land3, gz, gy2, gx, swap_buf,
    lr, lr_sib,
    in_sem, ex_sem, cot_sem, a2a_send, a2a_recv, red_send, red_recv,
    gi_loc, gi_send, gi_recv, lr_send, lr_recv, swap_send, swap_recv,
):
    me = lax.axis_index("blk")
    core = lax.axis_index("pipe")
    other = 1 - core
    sibling = {"pipe": other}
    px, pz, py = lax.div(me, NZ * NY), lax.rem(lax.div(me, NY), NZ), lax.rem(me, NY)

    local = (
        (x_in.at[core], x_buf), (left_in, left_buf), (right_in, right_buf),
        (first_in, first_buf), (second_in, second_buf),
    )
    for i, (src, dst) in enumerate(local):
        pltpu.make_async_copy(src, dst.at[core], in_sem.at[core, i]).start()
    cot_copy = pltpu.make_async_copy(cot_in.at[core], gy_buf, cot_sem)
    cot_copy.start()

    barrier = pltpu.get_barrier_semaphore()

    def greet(step, carry):
        peer = lax.rem(me + step, NB)
        pl.semaphore_signal(barrier, inc=1, device_id={"blk": peer}, device_id_type=MESH)
        return carry

    pl.semaphore_signal(barrier, inc=1, device_id=sibling, device_id_type=MESH)
    lax.fori_loop(1, NB, greet, 0)

    remote = (
        (x_in.at[other], x_buf), (left_in, left_buf), (right_in, right_buf),
        (first_in, first_buf), (second_in, second_buf),
    )

    def exchange_copy(i):
        src, dst = remote[i]
        return pltpu.make_async_remote_copy(
            src_ref=src, dst_ref=dst.at[core], send_sem=ex_sem.at[i], recv_sem=in_sem.at[core, i],
            device_id=sibling, device_id_type=MESH,
        )

    def await_input(section, i):
        ref = (x_buf, left_buf, right_buf, first_buf, second_buf)[i].at[section]
        pltpu.make_async_copy(ref, ref, in_sem.at[section, i]).wait()

    def all_to_all(src, dst, recv_id, send_id, lo, size, first=0, count=NB):
        columns = pl.ds(lo, size)

        def rows(i):
            return pl.ds(pl.multiple_of(2 * i, 2), 2)

        def send(step, carry):
            peer = lax.rem(me + step, NB)
            pltpu.make_async_remote_copy(
                src_ref=src.at[rows(peer), columns], dst_ref=dst.at[rows(me), columns],
                send_sem=a2a_send.at[send_id], recv_sem=a2a_recv.at[recv_id],
                device_id={"blk": peer}, device_id_type=MESH,
            ).start()
            return carry

        lax.fori_loop(max(first, 1), first + count, send, 0)
        if first == 0:
            pltpu.make_async_copy(
                src.at[rows(me), columns], dst.at[rows(me), columns], a2a_recv.at[recv_id]
            ).start()
            pltpu.make_async_copy(
                src.at[rows(me), columns], dummy.at[recv_id, :, columns], a2a_send.at[send_id]
            ).start()

    def await_block(ref, sem, ident, lo, size, rows=2 * T):
        part = ref.at[pl.ds(0, rows), pl.ds(lo, size)]
        pltpu.make_async_copy(part, part, sem.at[ident]).wait()

    def expand(section):
        row = lax.broadcasted_iota(jnp.int32, (2 * T, T), 0)
        col = lax.broadcasted_iota(jnp.int32, (2 * T, T), 1)
        left = left_buf[section]
        for h in range(2):
            spread = (row == 2 * col + h).astype(F32).astype(BF16)
            part = slice(h * T, (h + 1) * T)
            lexp[section, part, :] = mm(left, spread, 1, 1).astype(BF16)
            lexp_t[section, :, part] = mm(spread, left, 1, 1).astype(BF16)

    def expand_right(section):
        row = lax.broadcasted_iota(jnp.int32, (2 * T, T), 0)
        col = lax.broadcasted_iota(jnp.int32, (2 * T, T), 1)
        right = right_buf[section]
        for h in range(2):
            spread = (row == 2 * col + h).astype(F32).astype(BF16)
            part = slice(h * T, (h + 1) * T)
            rexp[section, :, part] = mm(spread, right).astype(BF16)

    def build_pairs(section):
        row = lax.broadcasted_iota(jnp.int32, (NK, T), 0)
        col = lax.broadcasted_iota(jnp.int32, (NK, T), 1)
        twice = ((col == row) | (col == row + NK)).astype(F32).astype(BF16)
        low = lax.broadcasted_iota(jnp.int32, (T, T), 0) < NK
        first_half = lax.broadcasted_iota(jnp.int32, (T, T), 1) < NK

        def step(b, carry):
            rows = aligned(b, T)
            both = mm(first_buf[section, rows, :], twice)
            pair_buf[section, rows, :] = jnp.where(low == first_half, both, 0.0).astype(BF16)
            return carry

        lax.fori_loop(0, NK // 2, step, 0, unroll=4)

    def gate(section, grad_out, sent, lo, size):
        def step(i, carry):
            off = lo + i * TILE
            cs = pl.ds(pl.multiple_of(off, TILE), TILE)
            for h in range(2):
                wide = pl.ds(pl.multiple_of(off + h * HALF, TILE), TILE)
                value = grad_out[:, wide].astype(F32) * x_buf[section, :, wide].astype(F32)
                gate_buf[h * T : (h + 1) * T, cs] = value.astype(BF16)
            sent[:, cs] = mm(lexp_t[section], gate_buf[:, cs]).astype(BF16)
            return carry

        lax.fori_loop(0, size // TILE, step, 0)

    def swap_blocks(src, dst, lo, size):
        ps = pl.ds(lo, size)

        def step(g, carry):
            qs = aligned(g, 16)
            dst[qs, ps, :] = jnp.swapaxes(src[ps, qs, :], 0, 1)
            return carry

        lax.fori_loop(0, NK // 16, step, 0)

    def forward(section, sent):
        def mixed(b, carry):
            cols = aligned(b, T)
            out = mm(pair_buf[section, cols, :], x_buf[section, :, cols], 1, 1)
            mt_buf[aligned(b, 2)] = out.astype(BF16).reshape(2, NK, T)
            return carry

        lax.fori_loop(0, NK // 2, mixed, 0, unroll=4)
        swap_blocks(mt_buf, mk_buf.at[section], 0, NK)

        def hidden(k, carry):
            rows = aligned(k, NK)
            for h in range(2):
                kk = k + h * (NK // 2)
                out = mm(second_buf[section, kk], mk_buf[section, kk])
                ht_buf[section, rows, h * T : (h + 1) * T] = out.astype(BF16)
            return carry

        lax.fori_loop(0, NK // 2, hidden, 0, unroll=4)

        def rows_of(i, carry):
            cs = aligned(i, TILE)
            sent[:, cs] = mm(rexp[section], ht_buf[section, cs, :], 1, 1).astype(BF16)
            return carry

        lax.fori_loop(0, HALF // TILE, rows_of, 0)

    def fold(target):
        even = lax.rem(lax.broadcasted_iota(jnp.int32, (2 * T, T), 0), 2) == 0
        tmp[...] = jnp.where(even, acc[:, :T], acc[:, T:])
        target[...] = tmp[pl.ds(0, T, stride=2), :] + tmp[pl.ds(1, T, stride=2), :]

    def channel_back(section, returned, part, parts):
        if part == 0:
            acc[...] = jnp.zeros_like(acc)
        tiles = HALF // TILE // parts
        pairs = NK // 4 // parts
        first_half = lax.broadcasted_iota(jnp.int32, (NK, T), 1) < NK

        def step(i, carry):
            cs = aligned(i, TILE)
            acc[...] += mm(returned[:, cs], ht_buf[section, cs, :])
            hg_buf[cs, :] = mm(returned[:, cs], rexp[section], 0, 0).astype(BF16)
            return carry

        lax.fori_loop(part * tiles, (part + 1) * tiles, step, 0)

        def pair(b, carry):
            for h in range(2):
                k0 = 2 * b + h * (NK // 2)
                grad = hg_buf[aligned(b, T), h * T : (h + 1) * T]
                mix = mk_buf[section, pl.ds(k0, 2)].reshape(T, T)
                outer = mm(grad, mix, 1, 1)
                grads[section, 1, pl.ds(pl.multiple_of(k0 * (NK // 2), NK), NK), :] = jnp.where(
                    first_half, outer[:NK], outer[NK:]
                )
                for q in range(2):
                    back = mm(second_buf[section, k0 + q], grad[q * NK : (q + 1) * NK], 0, 0)
                    mt_buf[k0 + q] = back.astype(BF16)
            return carry

        lax.fori_loop(part * pairs, (part + 1) * pairs, pair, 0, unroll=2)
        for h in range(2):
            swap_blocks(mt_buf, mg_view, h * (NK // 2) + part * 2 * pairs, 2 * pairs)
        if part < parts - 1:
            return
        fold(lr.at[section, 0])

        def columns(b, carry):
            cols = aligned(b, T)
            mixed_grad = mg_view[aligned(b, 2)].reshape(T, T)
            outer = mm(mixed_grad, x_buf[section, :, cols])
            grads[section, 0, aligned(b, NK), :] = jnp.where(first_half, outer[:NK], outer[NK:])
            cb_buf[:, cols] = mm(mixed_grad, pair_buf[section, cols, :], 0, 0)
            return carry

        lax.fori_loop(0, NK // 2, columns, 0, unroll=4)

    mg_view = mk_buf.at[2]

    def carry_out(section, gathered, grad_out, lo, size):
        def step(i, carry):
            off = lo + i * TILE
            cs = pl.ds(pl.multiple_of(off, TILE), TILE)
            block = gathered[:, cs]
            carried = mm(lexp[section], block)
            for h in range(2):
                wide = pl.ds(pl.multiple_of(off + h * HALF, TILE), TILE)
                value = grad_out[:, wide].astype(F32) * carried[h * T : (h + 1) * T] + cb_buf[:, wide]
                gi_buf[section, :, wide] = value.astype(BF16)
            acc[...] += mm(block, gate_buf[:, cs], 1, 1)
            return carry

        lax.fori_loop(0, size // TILE, step, 0)

    def finish_left(section):
        fold(tmp2)
        lr[section, 1] = tmp2[...].T

    tmp2 = acc2.at[2]

    def send_input_grad(section, lo, size):
        for h in range(2):
            cols = pl.ds(h * HALF + lo, size)
            src, dst = gi_buf.at[section, :, cols], gi_out.at[core, :, cols]

            @pl.when(core == section)
            def _():
                pltpu.make_async_copy(src, dst, gi_loc).start()

            @pl.when(core != section)
            def _():
                pltpu.make_async_remote_copy(
                    src_ref=src, dst_ref=dst, send_sem=gi_send, recv_sem=gi_recv,
                    device_id=sibling, device_id_type=MESH,
                ).start()

    is_low = core == 0
    coord1, coord2 = jnp.where(is_low, px, py), jnp.where(is_low, py, px)
    stride1, stride2 = jnp.where(is_low, NZ * NY, 1), jnp.where(is_low, 1, NZ * NY)
    axes = ((coord1, stride1, NX), (coord2, stride2, NY), (pz, NY, NZ))

    def hop(axis, d):
        coord, stride, size = axes[axis]
        return {"blk": me + (lax.rem(coord + d, size) - coord) * stride}

    def copies(section, base, axis, src_of, dst_of):
        size = axes[axis][2]
        return [
            pltpu.make_async_remote_copy(
                src_ref=src_of(d), dst_ref=dst_of(d),
                send_sem=red_send.at[section, base + d], recv_sem=red_recv.at[section, base + d],
                device_id=hop(axis, d), device_id_type=MESH,
            )
            for d in range(1, size)
        ]

    def scatter(section, base, axis, stage, landing):
        coord, _, size = axes[axis]
        rows = landing.shape[2]
        return copies(
            section, base, axis,
            lambda d: stage.at[section, aligned(lax.rem(coord + d, size), rows)],
            lambda d: landing.at[section, d],
        )

    def gather(section, base, axis, buf):
        coord = axes[axis][0]
        return copies(
            section, base, axis,
            lambda d: buf.at[section, coord],
            lambda d: buf.at[section, coord],
        )

    def sib_copy(section):
        return pltpu.make_async_remote_copy(
            src_ref=grads.at[section, other], dst_ref=sib.at[section],
            send_sem=red_send.at[section, 0], recv_sem=red_recv.at[section, 0],
            device_id=sibling, device_id_type=MESH,
        )

    def start(group):
        for c in group:
            c.start()

    def finish(group):
        for c in group:
            c.wait()

    def reduce_stage(section, number):
        def s1():
            return scatter(section, 0, 0, stage1, land1)

        def s2():
            return scatter(section, 3, 1, stage2, land2)

        def s3():
            return scatter(section, 6, 2, stage3, land3)

        def g3():
            return gather(section, 13, 2, gz)

        def g2():
            return gather(section, 20, 1, gy2)

        def g1():
            return gather(section, 23, 0, gx)

        def settle(values, coord, landing, size):
            rows = landing.shape[2]
            total = values[aligned(coord, rows), :]
            for d in range(1, size):
                total = total + landing[section, d].astype(F32)
            return total

        if number == 0:
            sib_copy(section).start()
        elif number == 1:
            sib_copy(section).wait()
            mine = grads.at[section, core]

            def add(i, carry):
                rows = aligned(i, 256)
                total = mine[rows, :] + sib[section, rows, :]
                sib[section, rows, :] = total
                stage1[section, rows, :] = total.astype(BF16)
                return carry

            lax.fori_loop(0, HR // 256, add, 0)
            start(s1())
        elif number == 2:
            finish(s1())
            value = settle(sib.at[section], coord1, land1, NX)
            acc1[section] = value
            stage2[section] = value.astype(BF16)
            start(s2())
        elif number == 3:
            finish(s2())
            value = settle(acc1.at[section], coord2, land2, NY)
            acc2[section] = value
            stage3[section] = value.astype(BF16)
            start(s3())
        elif number == 4:
            finish(s3())
            value = settle(acc2.at[section], pz, land3, NZ)
            gz[section, pz] = value.astype(BF16)
            start(g3())
        elif number == 5:
            finish(g3())
            gy2[section, coord2] = gz[section].reshape(T, T)
            start(g2())
        elif number == 6:
            finish(g2())
            gx[section, coord1] = gy2[section].reshape(NY * T, T)
            start(g1())
        else:
            finish(g1())

    def unpack(packed, out):
        def step(b, carry):
            block = packed(b).astype(F32)
            out[2 * b] = block[:, :NK]
            out[2 * b + 1] = block[:, NK:]
            return carry

        lax.fori_loop(0, NK // 2, step, 0, unroll=4)

    for i in range(5):
        await_input(core, i)
    expand(core)
    expand_right(core)
    build_pairs(core)
    cot_copy.wait()
    pl.semaphore_wait(barrier, NB)
    for i in (1, 0, 2, 3, 4):
        exchange_copy(i).start()
    await_input(other, 1)
    expand(other)

    @pl.when(core == 0)
    def _():
        await_input(1, 0)

    gate(1, gy_buf, send_b.at[1], 0, HALF)
    all_to_all(send_b.at[1], recv_b.at[1], 0, 0, 0, HALF)

    for i in (2, 3, 4):
        await_input(other, i)
    expand_right(other)
    build_pairs(other)
    forward(1, send_f.at[1])
    PART = HALF // 2
    for p in range(2):
        all_to_all(send_f.at[1], recv_f.at[1], 1 + p, 1 + p, p * PART, PART)

    @pl.when(core == 1)
    def _():
        await_input(0, 0)

    forward(0, send_f.at[0])

    await_block(recv_b.at[1], a2a_recv, 0, 0, HALF)
    channel_back(1, recv_b.at[1], 0, 1)
    reduce_stage(1, 0)
    reduce_stage(1, 1)

    acc[...] = jnp.zeros_like(acc)
    for p in range(2):
        await_block(recv_f.at[1], a2a_recv, 1 + p, p * PART, PART)
        carry_out(1, recv_f.at[1], gy_buf, p * PART, PART)
        gate(0, gi_buf.at[1], send_b.at[0], p * PART, PART)
        if p == 1:
            reduce_stage(1, 2)
        all_to_all(send_b.at[0], recv_b.at[0], 3 + p, 3 + p, p * PART, PART)
        send_input_grad(1, p * PART, PART)
    finish_left(1)

    GROUP = 32
    groups = [(p, g) for p in range(2) for g in range(NB // GROUP)]

    def pump(n):
        if n >= 2:
            p, g = groups[n - 2]
            await_block(send_f.at[0], a2a_send, 5 + n - 2, p * PART, PART, 2 * GROUP)
        if n < len(groups):
            p, g = groups[n]
            all_to_all(send_f.at[0], recv_f.at[0], 5 + p, 5 + n, p * PART, PART, g * GROUP, GROUP)

    await_block(recv_b.at[0], a2a_recv, 3, 0, PART)
    channel_back(0, recv_b.at[0], 0, 2)
    reduce_stage(1, 3)
    pump(0)
    pump(1)
    await_block(recv_b.at[0], a2a_recv, 4, PART, PART)
    channel_back(0, recv_b.at[0], 1, 2)
    reduce_stage(0, 0)
    pump(2)
    reduce_stage(1, 4)
    reduce_stage(0, 1)
    pump(3)
    reduce_stage(1, 5)
    pump(4)
    reduce_stage(0, 2)
    reduce_stage(1, 6)
    pump(5)
    acc[...] = jnp.zeros_like(acc)
    await_block(recv_f.at[0], a2a_recv, 5, 0, PART)
    carry_out(0, recv_f.at[0], gi_buf.at[1], 0, PART)
    send_input_grad(0, 0, PART)
    reduce_stage(0, 3)
    pump(6)
    reduce_stage(1, 7)
    reduce_stage(0, 4)
    pump(7)
    reduce_stage(0, 5)
    await_block(recv_f.at[0], a2a_recv, 6, PART, PART)
    carry_out(0, recv_f.at[0], gi_buf.at[1], PART, PART)
    send_input_grad(0, PART, PART)
    reduce_stage(0, 6)
    finish_left(0)
    lr_copy = pltpu.make_async_remote_copy(
        src_ref=lr.at[other], dst_ref=lr_sib, send_sem=lr_send, recv_sem=lr_recv,
        device_id=sibling, device_id_type=MESH,
    )
    lr_copy.start()
    reduce_stage(0, 7)
    swap_copy = pltpu.make_async_remote_copy(
        src_ref=gx.at[other], dst_ref=swap_buf, send_sem=swap_send, recv_sem=swap_recv,
        device_id=sibling, device_id_type=MESH,
    )
    swap_copy.start()

    def own_block(section):
        return lambda b: gx[section, lax.div(b, 8), pl.ds(pl.multiple_of(lax.rem(b, 8) * NK, NK), NK), :]

    def swap_block(b):
        return swap_buf[lax.div(b, 8), pl.ds(pl.multiple_of(lax.rem(b, 8) * NK, NK), NK), :]

    @pl.when(core == 0)
    def _():
        unpack(own_block(0), first_out)

    @pl.when(core == 1)
    def _():
        unpack(own_block(1), second_out)

    lr_copy.wait()
    right_out[...] = lr[core, 0] + lr_sib[0]
    left_out[...] = lr[core, 1] + lr_sib[1]
    swap_copy.wait()

    @pl.when(core == 0)
    def _():
        unpack(swap_block, second_out)

    @pl.when(core == 1)
    def _():
        unpack(swap_block, first_out)

    for i in range(5):
        exchange_copy(i).wait_send()
    await_block(send_b.at[1], a2a_send, 0, 0, HALF)
    for p in range(2):
        await_block(send_f.at[1], a2a_send, 1 + p, p * PART, PART)
        await_block(send_b.at[0], a2a_send, 3 + p, p * PART, PART)
    pump(8)
    pump(9)
    pltpu.make_async_copy(gi_buf.at[0], gi_out.at[0], gi_loc).wait()
    pltpu.make_async_copy(gi_buf.at[0], gi_out.at[0], gi_send).wait()
    pltpu.make_async_copy(gi_buf.at[0], gi_out.at[0], gi_recv).wait()


def body(x_saved, cotangent, seq_right, seq_left, chan_first, chan_second):
    v, dma = pltpu.VMEM, pltpu.SemaphoreType.DMA
    anywhere = pl.BlockSpec(memory_space=pl.ANY)
    vmem = pl.BlockSpec(memory_space=pltpu.VMEM)
    gi, right, left, first, second = pl.pallas_call(
        kernel,
        name="monarch_backward",
        out_shape=[
            jax.ShapeDtypeStruct((2, T, D), BF16),
            jax.ShapeDtypeStruct((T, T), F32),
            jax.ShapeDtypeStruct((T, T), F32),
            jax.ShapeDtypeStruct((NK, NK, NK), F32),
            jax.ShapeDtypeStruct((NK, NK, NK), F32),
        ],
        in_specs=[anywhere] * 6,
        out_specs=[anywhere, vmem, vmem, vmem, vmem],
        scratch_shapes=[
            v((2, T, D), BF16), v((2, T, T), BF16), v((2, T, T), BF16),
            v((2, D, NK), BF16), v((2, NK, NK, NK), BF16),
            v((T, D), BF16), v((2, T, D), BF16), v((2 * T, HALF), BF16), v((2, D, T), BF16),
            v((NK, NK, T), BF16), v((3, NK, NK, T), BF16), v((2, HALF, 2 * T), BF16),
            v((HALF, 2 * T), BF16), v((T, D), F32),
            v((2, 2 * T, 2 * T), BF16), v((2, 2 * T, 2 * T), BF16), v((2, 2 * T, 2 * T), BF16),
            v((2, 2 * T, HALF), BF16), v((2, 2 * T, HALF), BF16),
            v((2, 2 * T, HALF), BF16), v((2, 2 * T, HALF), BF16),
            v((7, 2, HALF), BF16), v((2 * T, 2 * T), F32), v((2 * T, T), F32),
            v((2, 2, HR, T), F32), v((2, HR, T), F32),
            v((2, HR, T), BF16), v((2, NX, HR // NX, T), BF16), v((2, HR // NX, T), F32),
            v((2, HR // NX, T), BF16), v((2, NY, T, T), BF16), v((3, T, T), F32),
            v((2, T, T), BF16), v((2, NZ, T // NZ, T), BF16),
            v((2, NZ, T // NZ, T), BF16), v((2, NY, T, T), BF16), v((2, NX, NY * T, T), BF16),
            v((NX, NY * T, T), BF16),
            v((2, 2, T, T), F32), v((2, T, T), F32),
            dma((2, 5)), dma((5,)), dma, dma((13,)), dma((7,)), dma((2, 27)), dma((2, 27)),
            dma, dma, dma, dma, dma, dma, dma,
        ],
        compiler_params=pltpu.CompilerParams(
            collective_id=1, has_side_effects=True, vmem_limit_bytes=64_000_000
        ),
    )(
        x_saved[0], cotangent, seq_right[0, 0], seq_left[0, 0],
        chan_first[0].reshape(D, NK), chan_second[0],
    )

    return (gi[None], right[None, None], left[None, None], first[None], second[None])


def solution(mesh):
    in_specs = (
        P("pipe", None, "blk", None),
        P(None, "blk", None),
        P("pipe", "blk", None, None),
        P("pipe", "blk", None, None),
        P("pipe", None, None, None),
        P("pipe", None, None, None),
    )
    out_specs = (
        P("pipe", None, "blk", None),
        P("pipe", "blk", None, None),
        P("pipe", "blk", None, None),
        P("pipe", None, None, None),
        P("pipe", None, None, None),
    )
    return jax.shard_map(body, mesh=mesh, in_specs=in_specs, out_specs=out_specs, check_vma=False)
```

```python
import jax
import jax.numpy as jnp
from jax import lax
from jax.experimental import pallas as pl
from jax.experimental.pallas import tpu as pltpu
from jax.sharding import PartitionSpec as P

MESH = pl.DeviceIdType.MESH
F32, BF16 = jnp.float32, jnp.bfloat16
NX, NZ, NY = 4, 8, 4
NB = NX * NZ * NY
T = 128
D = 4096
HALF = D // 2
NK = 64
TILE = 512
HR = 2048


def mm(a, b, ca=1, cb=0):
    return lax.dot_general(a, b, (((ca,), (cb,)), ((), ())), preferred_element_type=F32)


def aligned(index, size):
    return pl.ds(pl.multiple_of(index * size, size), size)


def kernel(
    x_in, cot_in, right_in, left_in, first_in, second_in,
    gi_out, right_out, left_out, first_out, second_out,
    x_buf, right_buf, left_buf, first_buf, second_buf,
    gy_buf, gi_buf, gate_buf, pair_buf, mt_buf, mk_buf, ht_buf, hg_buf, cb_buf,
    rexp, lexp, lexp_t,
    send_f, recv_f, send_b, recv_b, dummy, acc, tmp,
    grads, stage0, sib, stage1, land1, acc1, stage2, land2, total, gx, lr, lr_sib, left_sum,
    in_sem, ex_sem, cot_sem, a2a_send, a2a_recv, red_send, red_recv,
    gi_loc, gi_send, gi_recv, lr_send, lr_recv,
):
    me = lax.axis_index("blk")
    core = lax.axis_index("pipe")
    other = 1 - core
    sibling = {"pipe": other}
    px, pz, py = lax.div(me, NZ * NY), lax.rem(lax.div(me, NY), NZ), lax.rem(me, NY)

    local = (
        (x_in.at[core], x_buf), (left_in, left_buf), (right_in, right_buf),
        (first_in, first_buf), (second_in, second_buf),
    )
    for i, (src, dst) in enumerate(local):
        pltpu.make_async_copy(src, dst.at[core], in_sem.at[core, i]).start()
    cot_copy = pltpu.make_async_copy(cot_in.at[core], gy_buf, cot_sem)
    cot_copy.start()

    barrier = pltpu.get_barrier_semaphore()

    def greet(step, carry):
        peer = lax.rem(me + step, NB)
        pl.semaphore_signal(barrier, inc=1, device_id={"blk": peer}, device_id_type=MESH)
        return carry

    pl.semaphore_signal(barrier, inc=1, device_id=sibling, device_id_type=MESH)
    lax.fori_loop(1, NB, greet, 0)
    for d in range(1, NX):
        for axis_peer in (
            me + (lax.rem(px + d, NX) - px) * (NZ * NY),
            me + (lax.rem(py + d, NY) - py),
        ):
            pl.semaphore_signal(
                barrier, inc=1, device_id={"blk": axis_peer, "pipe": other}, device_id_type=MESH
            )

    remote = (
        (x_in.at[other], x_buf), (left_in, left_buf), (right_in, right_buf),
        (first_in, first_buf), (second_in, second_buf),
    )

    def exchange_copy(i):
        src, dst = remote[i]
        return pltpu.make_async_remote_copy(
            src_ref=src, dst_ref=dst.at[core], send_sem=ex_sem.at[i], recv_sem=in_sem.at[core, i],
            device_id=sibling, device_id_type=MESH,
        )

    def await_input(section, i):
        ref = (x_buf, left_buf, right_buf, first_buf, second_buf)[i].at[section]
        pltpu.make_async_copy(ref, ref, in_sem.at[section, i]).wait()

    def all_to_all(src, dst, recv_id, send_id, lo, size, first=0, count=NB):
        columns = pl.ds(lo, size)

        def rows(i):
            return pl.ds(pl.multiple_of(2 * i, 2), 2)

        def send(step, carry):
            peer = lax.rem(me + step, NB)
            pltpu.make_async_remote_copy(
                src_ref=src.at[rows(peer), columns], dst_ref=dst.at[rows(me), columns],
                send_sem=a2a_send.at[send_id], recv_sem=a2a_recv.at[recv_id],
                device_id={"blk": peer}, device_id_type=MESH,
            ).start()
            return carry

        lax.fori_loop(max(first, 1), first + count, send, 0)
        if first == 0:
            pltpu.make_async_copy(
                src.at[rows(me), columns], dst.at[rows(me), columns], a2a_recv.at[recv_id]
            ).start()
            pltpu.make_async_copy(
                src.at[rows(me), columns], dummy.at[recv_id, :, columns], a2a_send.at[send_id]
            ).start()

    def await_block(ref, sem, ident, lo, size, rows=2 * T):
        part = ref.at[pl.ds(0, rows), pl.ds(lo, size)]
        pltpu.make_async_copy(part, part, sem.at[ident]).wait()

    def expand(section):
        row = lax.broadcasted_iota(jnp.int32, (2 * T, T), 0)
        col = lax.broadcasted_iota(jnp.int32, (2 * T, T), 1)
        left = left_buf[section]
        for h in range(2):
            spread = (row == 2 * col + h).astype(F32).astype(BF16)
            part = slice(h * T, (h + 1) * T)
            lexp[section, part, :] = mm(left, spread, 1, 1).astype(BF16)
            lexp_t[section, :, part] = mm(spread, left, 1, 1).astype(BF16)

    def expand_right(section):
        row = lax.broadcasted_iota(jnp.int32, (2 * T, T), 0)
        col = lax.broadcasted_iota(jnp.int32, (2 * T, T), 1)
        right = right_buf[section]
        for h in range(2):
            spread = (row == 2 * col + h).astype(F32).astype(BF16)
            part = slice(h * T, (h + 1) * T)
            rexp[section, :, part] = mm(spread, right).astype(BF16)

    def build_pairs(section):
        row = lax.broadcasted_iota(jnp.int32, (NK, T), 0)
        col = lax.broadcasted_iota(jnp.int32, (NK, T), 1)
        twice = ((col == row) | (col == row + NK)).astype(F32).astype(BF16)
        low = lax.broadcasted_iota(jnp.int32, (T, T), 0) < NK
        first_half = lax.broadcasted_iota(jnp.int32, (T, T), 1) < NK

        def step(b, carry):
            rows = aligned(b, T)
            both = mm(first_buf[section, rows, :], twice)
            pair_buf[section, rows, :] = jnp.where(low == first_half, both, 0.0).astype(BF16)
            return carry

        lax.fori_loop(0, NK // 2, step, 0, unroll=4)

    def gate(section, grad_out, sent, lo, size):
        def step(i, carry):
            off = lo + i * TILE
            cs = pl.ds(pl.multiple_of(off, TILE), TILE)
            for h in range(2):
                wide = pl.ds(pl.multiple_of(off + h * HALF, TILE), TILE)
                value = grad_out[:, wide].astype(F32) * x_buf[section, :, wide].astype(F32)
                gate_buf[h * T : (h + 1) * T, cs] = value.astype(BF16)
            sent[:, cs] = mm(lexp_t[section], gate_buf[:, cs]).astype(BF16)
            return carry

        lax.fori_loop(0, size // TILE, step, 0)

    def swap_blocks(src, dst, lo, size):
        ps = pl.ds(lo, size)

        def step(g, carry):
            qs = aligned(g, 16)
            dst[qs, ps, :] = jnp.swapaxes(src[ps, qs, :], 0, 1)
            return carry

        lax.fori_loop(0, NK // 16, step, 0)

    def forward(section, sent):
        def mixed(b, carry):
            cols = aligned(b, T)
            out = mm(pair_buf[section, cols, :], x_buf[section, :, cols], 1, 1)
            mt_buf[aligned(b, 2)] = out.astype(BF16).reshape(2, NK, T)
            return carry

        lax.fori_loop(0, NK // 2, mixed, 0, unroll=4)
        swap_blocks(mt_buf, mk_buf.at[section], 0, NK)

        def hidden(k, carry):
            rows = aligned(k, NK)
            for h in range(2):
                kk = k + h * (NK // 2)
                out = mm(second_buf[section, kk], mk_buf[section, kk])
                ht_buf[section, rows, h * T : (h + 1) * T] = out.astype(BF16)
            return carry

        lax.fori_loop(0, NK // 2, hidden, 0, unroll=4)

        def rows_of(i, carry):
            cs = aligned(i, TILE)
            sent[:, cs] = mm(rexp[section], ht_buf[section, cs, :], 1, 1).astype(BF16)
            return carry

        lax.fori_loop(0, HALF // TILE, rows_of, 0)

    def fold(target):
        even = lax.rem(lax.broadcasted_iota(jnp.int32, (2 * T, T), 0), 2) == 0
        tmp[...] = jnp.where(even, acc[:, :T], acc[:, T:])
        target[...] = tmp[pl.ds(0, T, stride=2), :] + tmp[pl.ds(1, T, stride=2), :]

    def right_back(section, returned):
        acc[...] = jnp.zeros_like(acc)

        def step(i, carry):
            cs = aligned(i, TILE)
            acc[...] += mm(returned[:, cs], ht_buf[section, cs, :])
            return carry

        lax.fori_loop(0, HALF // TILE, step, 0)
        fold(lr.at[section, 0])

    def channel_back(section, returned, part, parts, between=lambda: None):
        tiles = HALF // TILE // parts
        pairs = NK // 4 // parts
        first_half = lax.broadcasted_iota(jnp.int32, (NK, T), 1) < NK

        def step(i, carry):
            cs = aligned(i, TILE)
            hg_buf[cs, :] = mm(returned[:, cs], rexp[section], 0, 0).astype(BF16)
            return carry

        lax.fori_loop(part * tiles, (part + 1) * tiles, step, 0)

        def pair(b, carry):
            for h in range(2):
                k0 = 2 * b + h * (NK // 2)
                grad = hg_buf[aligned(b, T), h * T : (h + 1) * T]
                mix = mk_buf[section, pl.ds(k0, 2)].reshape(T, T)
                outer = mm(grad, mix, 1, 1)
                grads[section, 1, pl.ds(pl.multiple_of(k0 * (NK // 2), NK), NK), :] = jnp.where(
                    first_half, outer[:NK], outer[NK:]
                )
                for q in range(2):
                    back = mm(second_buf[section, k0 + q], grad[q * NK : (q + 1) * NK], 0, 0)
                    mt_buf[k0 + q] = back.astype(BF16)
            return carry

        lax.fori_loop(part * pairs, (part + 1) * pairs, pair, 0, unroll=2)
        for h in range(2):
            swap_blocks(mt_buf, mg_view, h * (NK // 2) + part * 2 * pairs, 2 * pairs)
        if part < parts - 1:
            return
        between()

        def columns(b, carry):
            cols = aligned(b, T)
            mixed_grad = mg_view[aligned(b, 2)].reshape(T, T)
            outer = mm(mixed_grad, x_buf[section, :, cols])
            grads[section, 0, aligned(b, NK), :] = jnp.where(first_half, outer[:NK], outer[NK:])
            return carry

        lax.fori_loop(0, NK // 2, columns, 0, unroll=4)

    def channel_out(section):
        def columns(b, carry):
            cols = aligned(b, T)
            mixed_grad = mg_view[aligned(b, 2)].reshape(T, T)
            cb_buf[:, cols] = mm(mixed_grad, pair_buf[section, cols, :], 0, 0)
            return carry

        lax.fori_loop(0, NK // 2, columns, 0, unroll=4)

    mg_view = mk_buf.at[2]

    def carry_out(section, gathered, grad_out, lo, size):
        def step(i, carry):
            off = lo + i * TILE
            cs = pl.ds(pl.multiple_of(off, TILE), TILE)
            block = gathered[:, cs]
            carried = mm(lexp[section], block)
            for h in range(2):
                wide = pl.ds(pl.multiple_of(off + h * HALF, TILE), TILE)
                value = grad_out[:, wide].astype(F32) * carried[h * T : (h + 1) * T] + cb_buf[:, wide]
                gi_buf[section, :, wide] = value.astype(BF16)
            acc[...] += mm(block, gate_buf[:, cs], 1, 1)
            return carry

        lax.fori_loop(0, size // TILE, step, 0)

    def finish_left(section):
        fold(left_sum)
        lr[section, 1] = left_sum[...].T

    def send_input_grad(section, lo, size):
        for h in range(2):
            cols = pl.ds(h * HALF + lo, size)
            src, dst = gi_buf.at[section, :, cols], gi_out.at[core, :, cols]

            @pl.when(core == section)
            def _():
                pltpu.make_async_copy(src, dst, gi_loc).start()

            @pl.when(core != section)
            def _():
                pltpu.make_async_remote_copy(
                    src_ref=src, dst_ref=dst, send_sem=gi_send, recv_sem=gi_recv,
                    device_id=sibling, device_id_type=MESH,
                ).start()

    is_low = core == 0
    coord1, coord2 = jnp.where(is_low, px, py), jnp.where(is_low, py, px)
    stride1, stride2 = jnp.where(is_low, NZ * NY, 1), jnp.where(is_low, 1, NZ * NY)
    PIECE = HR // NX
    PLANE = NY * NZ
    SUB = PIECE // PLANE

    def hop(d):
        return me + (lax.rem(coord1 + d, NX) - coord1) * stride1

    def sib_copy(section, d):
        return pltpu.make_async_remote_copy(
            src_ref=stage0.at[section, d], dst_ref=sib.at[section, d],
            send_sem=red_send.at[section, d], recv_sem=red_recv.at[section, d],
            device_id=sibling, device_id_type=MESH,
        )

    def first_copy(section, d):
        return pltpu.make_async_remote_copy(
            src_ref=stage1.at[section, d], dst_ref=land1.at[section, d],
            send_sem=red_send.at[section, 4 + d], recv_sem=red_recv.at[section, 4 + d],
            device_id={"blk": hop(d)}, device_id_type=MESH,
        )

    def plane(u):
        return lax.rem(coord2 + lax.div(u, NZ), NY), lax.rem(pz + lax.rem(u, NZ), NZ)

    def plane_copy(section, u, src, dst, sem):
        c2, cz = plane(u)
        peer = me + (c2 - coord2) * stride2 + (cz - pz) * NY
        return pltpu.make_async_remote_copy(
            src_ref=src, dst_ref=dst, send_sem=red_send.at[section, sem], recv_sem=red_recv.at[section, sem],
            device_id={"blk": peer}, device_id_type=MESH,
        )

    def await_plane(ref, section, sem):
        part = ref.at[section, pl.ds(0, PLANE - 1)]
        pltpu.make_async_copy(part, part, red_send.at[section, sem]).wait()
        pltpu.make_async_copy(part, part, red_recv.at[section, sem]).wait()

    def last_copy(section, d):
        return pltpu.make_async_remote_copy(
            src_ref=total.at[section], dst_ref=gx.at[core, coord1],
            send_sem=red_send.at[section, 10 + d], recv_sem=red_recv.at[section, 10 + NX * core + d],
            device_id={"blk": hop(d), "pipe": section}, device_id_type=MESH,
        )

    def reduce_siblings(section):
        for d in (1, 2, 3, 0):
            rows = aligned(lax.rem(coord2 + d, NX), PIECE)
            stage0[section, d] = grads[section, other, rows, :].astype(BF16)
            sib_copy(section, d).start()

    def reduce_first(section):
        for d in (1, 2, 3, 0):
            rows = aligned(lax.rem(coord1 + d, NX), PIECE)
            sib_copy(section, d).wait()
            value = grads[section, core, rows, :] + sib[section, d].astype(F32)
            if d:
                stage1[section, d] = value.astype(BF16)
                first_copy(section, d).start()
            else:
                acc1[section] = value

    def reduce_plane(section):
        for d in range(1, NX):
            first_copy(section, d).wait()
        value = acc1[section]
        for d in range(1, NX):
            value = value + land1[section, d].astype(F32)
        acc1[section] = value
        stage2[section] = value.astype(BF16).reshape(PLANE, SUB, T)

        def send(u, carry):
            c2, cz = plane(u)
            plane_copy(section, u, stage2.at[section, c2 * NZ + cz], land2.at[section, u - 1], 8).start()
            return carry

        lax.fori_loop(1, PLANE, send, 0)

    def gather_plane(section):
        mine = coord2 * NZ + pz
        await_plane(land2, section, 8)

        def add(u, value):
            return value + land2[section, u].astype(F32)

        value = lax.fori_loop(0, PLANE - 1, add, acc1[section, aligned(mine, SUB), :], unroll=True)
        total[section, mine] = value.astype(BF16)

        def send(u, carry):
            plane_copy(section, u, total.at[section, mine], total.at[section, mine], 9).start()
            return carry

        lax.fori_loop(1, PLANE, send, 0)

    def gather_last(section):
        await_plane(total, section, 9)
        for d in range(1, NX):
            last_copy(section, d).start()

        @pl.when(core == section)
        def _():
            pltpu.make_async_copy(
                total.at[section], gx.at[core, coord1], red_recv.at[section, 10 + NX * core]
            ).start()

        @pl.when(core != section)
        def _():
            last_copy(section, 0).start()

    def await_last():
        for h in range(2):
            for d in range(NX):
                part = gx.at[h, d]
                pltpu.make_async_copy(part, part, red_recv.at[core, 10 + NX * h + d]).wait()

    def await_last_sends():
        for section in range(2):
            for d in range(1, NX):
                last_copy(section, d).wait_send()

            @pl.when(core != section)
            def _():
                last_copy(section, 0).wait_send()

    def unpack(half, out):
        def step(b, carry):
            rows = aligned(lax.rem(b, 8), 4)
            block = gx[half, lax.div(b, 8), rows].reshape(NK, T).astype(F32)
            out[2 * b] = block[:, :NK]
            out[2 * b + 1] = block[:, NK:]
            return carry

        lax.fori_loop(0, NK // 2, step, 0, unroll=4)

    for i in range(5):
        await_input(core, i)
    expand(core)
    expand_right(core)
    build_pairs(core)
    cot_copy.wait()
    pl.semaphore_wait(barrier, NB + NX + NY - 2)
    for i in (1, 0, 2, 3, 4):
        exchange_copy(i).start()
    await_input(other, 1)
    expand(other)

    @pl.when(core == 0)
    def _():
        await_input(1, 0)

    gate(1, gy_buf, send_b.at[1], 0, HALF)
    all_to_all(send_b.at[1], recv_b.at[1], 0, 0, 0, HALF)

    for i in (2, 3, 4):
        await_input(other, i)
    expand_right(other)
    build_pairs(other)
    forward(1, send_f.at[1])
    PART = HALF // 2
    for p in range(2):
        all_to_all(send_f.at[1], recv_f.at[1], 1 + p, 1 + p, p * PART, PART)

    @pl.when(core == 1)
    def _():
        await_input(0, 0)

    forward(0, send_f.at[0])

    await_block(recv_b.at[1], a2a_recv, 0, 0, HALF)
    channel_back(1, recv_b.at[1], 0, 1)
    reduce_siblings(1)
    channel_out(1)
    reduce_first(1)
    right_back(1, recv_b.at[1])

    acc[...] = jnp.zeros_like(acc)
    for p in range(2):
        await_block(recv_f.at[1], a2a_recv, 1 + p, p * PART, PART)
        carry_out(1, recv_f.at[1], gy_buf, p * PART, PART)
        gate(0, gi_buf.at[1], send_b.at[0], p * PART, PART)
        if p == 1:
            reduce_plane(1)
        all_to_all(send_b.at[0], recv_b.at[0], 3 + p, 3 + p, p * PART, PART)
        send_input_grad(1, p * PART, PART)
    finish_left(1)

    GROUP = 32
    groups = [(p, g) for p in range(2) for g in range(NB // GROUP)]

    def pump(n):
        if n >= 2:
            p, g = groups[n - 2]
            await_block(send_f.at[0], a2a_send, 5 + n - 2, p * PART, PART, 2 * GROUP)
        if n < len(groups):
            p, g = groups[n]
            all_to_all(send_f.at[0], recv_f.at[0], 5 + p, 5 + n, p * PART, PART, g * GROUP, GROUP)

    await_block(recv_b.at[0], a2a_recv, 3, 0, PART)
    channel_back(0, recv_b.at[0], 0, 2)
    gather_plane(1)
    pump(0)
    pump(1)
    await_block(recv_b.at[0], a2a_recv, 4, PART, PART)


    def between():
        gather_last(1)
        pump(2)

    channel_back(0, recv_b.at[0], 1, 2, between)
    reduce_siblings(0)
    channel_out(0)
    reduce_first(0)
    pump(3)
    right_back(0, recv_b.at[0])
    reduce_plane(0)
    pump(4)
    pump(5)
    gather_plane(0)
    pump(6)
    pump(7)
    acc[...] = jnp.zeros_like(acc)
    await_block(recv_f.at[0], a2a_recv, 5, 0, PART)
    carry_out(0, recv_f.at[0], gi_buf.at[1], 0, PART)
    send_input_grad(0, 0, PART)
    gather_last(0)
    await_block(recv_f.at[0], a2a_recv, 6, PART, PART)
    carry_out(0, recv_f.at[0], gi_buf.at[1], PART, PART)
    send_input_grad(0, PART, PART)
    finish_left(0)
    lr_copy = pltpu.make_async_remote_copy(
        src_ref=lr.at[other], dst_ref=lr_sib, send_sem=lr_send, recv_sem=lr_recv,
        device_id=sibling, device_id_type=MESH,
    )
    lr_copy.start()
    await_last()
    unpack(0, first_out)
    unpack(1, second_out)
    lr_copy.wait()
    right_out[...] = lr[core, 0] + lr_sib[0]
    left_out[...] = lr[core, 1] + lr_sib[1]
    await_last_sends()

    for i in range(5):
        exchange_copy(i).wait_send()
    await_block(send_b.at[1], a2a_send, 0, 0, HALF)
    for p in range(2):
        await_block(send_f.at[1], a2a_send, 1 + p, p * PART, PART)
        await_block(send_b.at[0], a2a_send, 3 + p, p * PART, PART)
    pump(8)
    pump(9)
    pltpu.make_async_copy(gi_buf.at[0], gi_out.at[0], gi_loc).wait()
    pltpu.make_async_copy(gi_buf.at[0], gi_out.at[0], gi_send).wait()
    pltpu.make_async_copy(gi_buf.at[0], gi_out.at[0], gi_recv).wait()


def body(x_saved, cotangent, seq_right, seq_left, chan_first, chan_second):
    v, dma = pltpu.VMEM, pltpu.SemaphoreType.DMA
    anywhere = pl.BlockSpec(memory_space=pl.ANY)
    vmem = pl.BlockSpec(memory_space=pltpu.VMEM)
    gi, right, left, first, second = pl.pallas_call(
        kernel,
        name="monarch_backward",
        out_shape=[
            jax.ShapeDtypeStruct((2, T, D), BF16),
            jax.ShapeDtypeStruct((T, T), F32),
            jax.ShapeDtypeStruct((T, T), F32),
            jax.ShapeDtypeStruct((NK, NK, NK), F32),
            jax.ShapeDtypeStruct((NK, NK, NK), F32),
        ],
        in_specs=[anywhere] * 6,
        out_specs=[vmem] * 5,
        scratch_shapes=[
            v((2, T, D), BF16), v((2, T, T), BF16), v((2, T, T), BF16),
            v((2, D, NK), BF16), v((2, NK, NK, NK), BF16),
            v((T, D), BF16), v((2, T, D), BF16), v((2 * T, HALF), BF16), v((2, D, T), BF16),
            v((NK, NK, T), BF16), v((3, NK, NK, T), BF16), v((2, HALF, 2 * T), BF16),
            v((HALF, 2 * T), BF16), v((T, D), F32),
            v((2, 2 * T, 2 * T), BF16), v((2, 2 * T, 2 * T), BF16), v((2, 2 * T, 2 * T), BF16),
            v((2, 2 * T, HALF), BF16), v((2, 2 * T, HALF), BF16),
            v((2, 2 * T, HALF), BF16), v((2, 2 * T, HALF), BF16),
            v((7, 2, HALF), BF16), v((2 * T, 2 * T), F32), v((2 * T, T), F32),
            v((2, 2, HR, T), F32), v((2, NX, HR // NX, T), BF16), v((2, NX, HR // NX, T), BF16),
            v((2, NX, HR // NX, T), BF16), v((2, NX, HR // NX, T), BF16), v((2, HR // NX, T), F32),
            v((2, NY * NZ, HR // NB, T), BF16), v((2, NY * NZ, HR // NB, T), BF16),
            v((2, NY * NZ, HR // NB, T), BF16), v((2, NX, NY * NZ, HR // NB, T), BF16),
            v((2, 2, T, T), F32), v((2, T, T), F32), v((T, T), F32),
            dma((2, 5)), dma((5,)), dma, dma((13,)), dma((7,)), dma((2, 18)), dma((2, 18)),
            dma, dma, dma, dma, dma,
        ],
        compiler_params=pltpu.CompilerParams(
            collective_id=1, has_side_effects=True, vmem_limit_bytes=64_000_000
        ),
    )(
        x_saved[0], cotangent, seq_right[0, 0], seq_left[0, 0],
        chan_first[0].reshape(D, NK), chan_second[0],
    )

    return (gi[None], right[None, None], left[None, None], first[None], second[None])


def solution(mesh):
    in_specs = (
        P("pipe", None, "blk", None),
        P(None, "blk", None),
        P("pipe", "blk", None, None),
        P("pipe", "blk", None, None),
        P("pipe", None, None, None),
        P("pipe", None, None, None),
    )
    out_specs = (
        P("pipe", None, "blk", None),
        P("pipe", "blk", None, None),
        P("pipe", "blk", None, None),
        P("pipe", None, None, None),
        P("pipe", None, None, None),
    )
    return jax.shard_map(body, mesh=mesh, in_specs=in_specs, out_specs=out_specs, check_vma=False)
```

```python
import jax
import jax.numpy as jnp
from jax import lax
from jax.experimental import pallas as pl
from jax.experimental.pallas import tpu as pltpu
from jax.sharding import PartitionSpec as P

MESH = pl.DeviceIdType.MESH
F32, BF16 = jnp.float32, jnp.bfloat16
NX, NZ, NY = 4, 8, 4
NB = NX * NZ * NY
T = 128
D = 4096
HALF = D // 2
NK = 64
TILE = 512
HR = 2048


def mm(a, b, ca=1, cb=0):
    return lax.dot_general(a, b, (((ca,), (cb,)), ((), ())), preferred_element_type=F32)


def aligned(index, size):
    return pl.ds(pl.multiple_of(index * size, size), size)


def kernel(
    x_in, cot_in, right_in, left_in, first_in, second_in,
    gi_own, gi_sib, right_out, left_out, first_out, second_out,
    x_buf, right_buf, left_buf, first_buf, second_buf,
    gy_buf, gi_buf, gate_buf, pair_buf, mt_buf, mk_buf, ht_buf, hg_buf, cb_buf,
    rexp, lexp, lexp_t,
    send_f, recv_f, send_b, recv_b, dummy, acc, tmp,
    grads, stage0, sib, stage1, land1, acc1, stage2, land2, total, gx, lr, lr_sib, left_sum,
    in_sem, ex_sem, cot_sem, a2a_send, a2a_recv, red_send, red_recv,
    gi_loc, gi_send, gi_recv, lr_send, lr_recv,
):
    me = lax.axis_index("blk")
    core = lax.axis_index("pipe")
    other = 1 - core
    sibling = {"pipe": other}
    px, pz, py = lax.div(me, NZ * NY), lax.rem(lax.div(me, NY), NZ), lax.rem(me, NY)

    local = (
        (x_in.at[core], x_buf), (left_in, left_buf), (right_in, right_buf),
        (first_in, first_buf), (second_in, second_buf),
    )
    for i, (src, dst) in enumerate(local):
        pltpu.make_async_copy(src, dst.at[core], in_sem.at[core, i]).start()
    cot_copy = pltpu.make_async_copy(cot_in.at[core], gy_buf, cot_sem)
    cot_copy.start()

    barrier = pltpu.get_barrier_semaphore()

    def greet(step, carry):
        peer = lax.rem(me + step, NB)
        pl.semaphore_signal(barrier, inc=1, device_id={"blk": peer}, device_id_type=MESH)
        return carry

    pl.semaphore_signal(barrier, inc=1, device_id=sibling, device_id_type=MESH)
    lax.fori_loop(1, NB, greet, 0)
    for d in range(1, NX):
        for axis_peer in (
            me + (lax.rem(px + d, NX) - px) * (NZ * NY),
            me + (lax.rem(py + d, NY) - py),
        ):
            pl.semaphore_signal(
                barrier, inc=1, device_id={"blk": axis_peer, "pipe": other}, device_id_type=MESH
            )

    remote = (
        (x_in.at[other], x_buf), (left_in, left_buf), (right_in, right_buf),
        (first_in, first_buf), (second_in, second_buf),
    )

    def exchange_copy(i):
        src, dst = remote[i]
        return pltpu.make_async_remote_copy(
            src_ref=src, dst_ref=dst.at[core], send_sem=ex_sem.at[i], recv_sem=in_sem.at[core, i],
            device_id=sibling, device_id_type=MESH,
        )

    def await_input(section, i):
        ref = (x_buf, left_buf, right_buf, first_buf, second_buf)[i].at[section]
        pltpu.make_async_copy(ref, ref, in_sem.at[section, i]).wait()

    def all_to_all(src, dst, recv_id, send_id, lo, size, first=0, count=NB, extra=None):
        columns = pl.ds(lo, size)

        def rows(i):
            return pl.ds(pl.multiple_of(2 * i, 2), 2)

        def send(step, carry):
            peer = lax.rem(me + step, NB)
            pltpu.make_async_remote_copy(
                src_ref=src.at[rows(peer), columns], dst_ref=dst.at[rows(me), columns],
                send_sem=a2a_send.at[send_id], recv_sem=a2a_recv.at[recv_id],
                device_id={"blk": peer}, device_id_type=MESH,
            ).start()
            if extra is not None:
                extra(step - first)
            return carry

        lax.fori_loop(max(first, 1), first + count, send, 0)
        if first == 0:
            if extra is not None:
                extra(jnp.int32(0))
            pltpu.make_async_copy(
                src.at[rows(me), columns], dst.at[rows(me), columns], a2a_recv.at[recv_id]
            ).start()
            pltpu.make_async_copy(
                src.at[rows(me), columns], dummy.at[recv_id, :, columns], a2a_send.at[send_id]
            ).start()

    def await_block(ref, sem, ident, lo, size, rows=2 * T):
        part = ref.at[pl.ds(0, rows), pl.ds(lo, size)]
        pltpu.make_async_copy(part, part, sem.at[ident]).wait()

    def expand(section):
        row = lax.broadcasted_iota(jnp.int32, (2 * T, T), 0)
        col = lax.broadcasted_iota(jnp.int32, (2 * T, T), 1)
        left = left_buf[section]
        for h in range(2):
            spread = (row == 2 * col + h).astype(F32).astype(BF16)
            part = slice(h * T, (h + 1) * T)
            lexp[section, part, :] = mm(left, spread, 1, 1).astype(BF16)
            lexp_t[section, :, part] = mm(spread, left, 1, 1).astype(BF16)

    def expand_right(section):
        row = lax.broadcasted_iota(jnp.int32, (2 * T, T), 0)
        col = lax.broadcasted_iota(jnp.int32, (2 * T, T), 1)
        right = right_buf[section]
        for h in range(2):
            spread = (row == 2 * col + h).astype(F32).astype(BF16)
            part = slice(h * T, (h + 1) * T)
            rexp[section, :, part] = mm(spread, right).astype(BF16)

    def build_pairs(section):
        row = lax.broadcasted_iota(jnp.int32, (NK, T), 0)
        col = lax.broadcasted_iota(jnp.int32, (NK, T), 1)
        twice = ((col == row) | (col == row + NK)).astype(F32).astype(BF16)
        low = lax.broadcasted_iota(jnp.int32, (T, T), 0) < NK
        first_half = lax.broadcasted_iota(jnp.int32, (T, T), 1) < NK

        def step(b, carry):
            rows = aligned(b, T)
            both = mm(first_buf[section, rows, :], twice)
            pair_buf[section, rows, :] = jnp.where(low == first_half, both, 0.0).astype(BF16)
            return carry

        lax.fori_loop(0, NK // 2, step, 0, unroll=4)

    def gate(section, grad_out, sent, lo, size):
        def step(i, carry):
            off = lo + i * TILE
            cs = pl.ds(pl.multiple_of(off, TILE), TILE)
            for h in range(2):
                wide = pl.ds(pl.multiple_of(off + h * HALF, TILE), TILE)
                value = grad_out[:, wide].astype(F32) * x_buf[section, :, wide].astype(F32)
                gate_buf[h * T : (h + 1) * T, cs] = value.astype(BF16)
            sent[:, cs] = mm(lexp_t[section], gate_buf[:, cs]).astype(BF16)
            return carry

        lax.fori_loop(0, size // TILE, step, 0)

    def swap_blocks(src, dst, lo, size):
        ps = pl.ds(lo, size)

        def step(g, carry):
            qs = aligned(g, 16)
            dst[qs, ps, :] = jnp.swapaxes(src[ps, qs, :], 0, 1)
            return carry

        lax.fori_loop(0, NK // 16, step, 0)

    def forward(section, sent):
        def mixed(b, carry):
            cols = aligned(b, T)
            out = mm(pair_buf[section, cols, :], x_buf[section, :, cols], 1, 1)
            mt_buf[aligned(b, 2)] = out.astype(BF16).reshape(2, NK, T)
            return carry

        lax.fori_loop(0, NK // 2, mixed, 0, unroll=4)
        swap_blocks(mt_buf, mk_buf.at[section], 0, NK)

        def hidden(k, carry):
            rows = aligned(k, NK)
            for h in range(2):
                kk = k + h * (NK // 2)
                out = mm(second_buf[section, kk], mk_buf[section, kk])
                ht_buf[section, rows, h * T : (h + 1) * T] = out.astype(BF16)
            return carry

        lax.fori_loop(0, NK // 2, hidden, 0, unroll=4)

        def rows_of(i, carry):
            cs = aligned(i, TILE)
            sent[:, cs] = mm(rexp[section], ht_buf[section, cs, :], 1, 1).astype(BF16)
            return carry

        lax.fori_loop(0, HALF // TILE, rows_of, 0)

    def fold(target):
        even = lax.rem(lax.broadcasted_iota(jnp.int32, (2 * T, T), 0), 2) == 0
        tmp[...] = jnp.where(even, acc[:, :T], acc[:, T:])
        target[...] = tmp[pl.ds(0, T, stride=2), :] + tmp[pl.ds(1, T, stride=2), :]

    def right_back(section, returned):
        acc[...] = jnp.zeros_like(acc)

        def step(i, carry):
            cs = aligned(i, TILE)
            acc[...] += mm(returned[:, cs], ht_buf[section, cs, :])
            return carry

        lax.fori_loop(0, HALF // TILE, step, 0)
        fold(lr.at[section, 0])

    def channel_back(section, returned, part, parts, between=lambda: None):
        tiles = HALF // TILE // parts
        pairs = NK // 4 // parts
        first_half = lax.broadcasted_iota(jnp.int32, (NK, T), 1) < NK

        def step(i, carry):
            cs = aligned(i, TILE)
            hg_buf[cs, :] = mm(returned[:, cs], rexp[section], 0, 0).astype(BF16)
            return carry

        lax.fori_loop(part * tiles, (part + 1) * tiles, step, 0)

        def pair(b, carry):
            for h in range(2):
                k0 = 2 * b + h * (NK // 2)
                grad = hg_buf[aligned(b, T), h * T : (h + 1) * T]
                mix = mk_buf[section, pl.ds(k0, 2)].reshape(T, T)
                outer = mm(grad, mix, 1, 1)
                grads[section, 1, pl.ds(pl.multiple_of(k0 * (NK // 2), NK), NK), :] = jnp.where(
                    first_half, outer[:NK], outer[NK:]
                )
                for q in range(2):
                    back = mm(second_buf[section, k0 + q], grad[q * NK : (q + 1) * NK], 0, 0)
                    mt_buf[k0 + q] = back.astype(BF16)
            return carry

        lax.fori_loop(part * pairs, (part + 1) * pairs, pair, 0, unroll=2)
        for h in range(2):
            swap_blocks(mt_buf, mg_view, h * (NK // 2) + part * 2 * pairs, 2 * pairs)
        if part < parts - 1:
            return
        between()

        def columns(b, carry):
            cols = aligned(b, T)
            mixed_grad = mg_view[aligned(b, 2)].reshape(T, T)
            outer = mm(mixed_grad, x_buf[section, :, cols])
            grads[section, 0, aligned(b, NK), :] = jnp.where(first_half, outer[:NK], outer[NK:])
            return carry

        lax.fori_loop(0, NK // 2, columns, 0, unroll=4)

    def channel_out(section):
        def columns(b, carry):
            cols = aligned(b, T)
            mixed_grad = mg_view[aligned(b, 2)].reshape(T, T)
            cb_buf[:, cols] = mm(mixed_grad, pair_buf[section, cols, :], 0, 0)
            return carry

        lax.fori_loop(0, NK // 2, columns, 0, unroll=4)

    mg_view = mk_buf.at[2]

    def carry_out(section, gathered, grad_out, lo, size):
        def step(i, carry):
            off = lo + i * TILE
            cs = pl.ds(pl.multiple_of(off, TILE), TILE)
            block = gathered[:, cs]
            carried = mm(lexp[section], block)
            for h in range(2):
                wide = pl.ds(pl.multiple_of(off + h * HALF, TILE), TILE)
                value = grad_out[:, wide].astype(F32) * carried[h * T : (h + 1) * T] + cb_buf[:, wide]
                gi_buf[section, :, wide] = value.astype(BF16)
            acc[...] += mm(block, gate_buf[:, cs], 1, 1)
            return carry

        lax.fori_loop(0, size // TILE, step, 0)

    def finish_left(section):
        fold(left_sum)
        lr[section, 1] = left_sum[...].T

    def send_input_grad(section, lo, size):
        for h in range(2):
            cols = pl.ds(h * HALF + lo, size)
            src = gi_buf.at[section, :, cols]

            @pl.when(core == section)
            def _():
                pltpu.make_async_copy(src, gi_own.at[:, cols], gi_loc).start()

            @pl.when(core != section)
            def _():
                pltpu.make_async_remote_copy(
                    src_ref=src, dst_ref=gi_sib.at[:, cols], send_sem=gi_send, recv_sem=gi_recv,
                    device_id=sibling, device_id_type=MESH,
                ).start()

    is_low = core == 0
    coord1, coord2 = jnp.where(is_low, px, py), jnp.where(is_low, py, px)
    stride1, stride2 = jnp.where(is_low, NZ * NY, 1), jnp.where(is_low, 1, NZ * NY)
    GROUP = 32
    PIECE = HR // NX
    PLANE = NY * NZ
    SUB = PIECE // PLANE

    def hop(d):
        return me + (lax.rem(coord1 + d, NX) - coord1) * stride1

    def sib_copy(section, d):
        return pltpu.make_async_remote_copy(
            src_ref=stage0.at[section, d], dst_ref=sib.at[section, d],
            send_sem=red_send.at[section, d], recv_sem=red_recv.at[section, d],
            device_id=sibling, device_id_type=MESH,
        )

    def first_copy(section, d):
        return pltpu.make_async_remote_copy(
            src_ref=stage1.at[section, d], dst_ref=land1.at[section, d],
            send_sem=red_send.at[section, 4 + d], recv_sem=red_recv.at[section, 4 + d],
            device_id={"blk": hop(d)}, device_id_type=MESH,
        )

    def plane(u):
        return lax.rem(coord2 + lax.div(u, NZ), NY), lax.rem(pz + lax.rem(u, NZ), NZ)

    def plane_copy(section, u, src, dst, sem):
        c2, cz = plane(u)
        peer = me + (c2 - coord2) * stride2 + (cz - pz) * NY
        return pltpu.make_async_remote_copy(
            src_ref=src, dst_ref=dst, send_sem=red_send.at[section, sem], recv_sem=red_recv.at[section, sem],
            device_id={"blk": peer}, device_id_type=MESH,
        )

    def await_plane(ref, section, sem):
        part = ref.at[section, pl.ds(0, PLANE - 1)]
        pltpu.make_async_copy(part, part, red_send.at[section, sem]).wait()
        pltpu.make_async_copy(part, part, red_recv.at[section, sem]).wait()

    def last_copy(section, d):
        return pltpu.make_async_remote_copy(
            src_ref=total.at[section], dst_ref=gx.at[core, coord1],
            send_sem=red_send.at[section, 10 + d], recv_sem=red_recv.at[section, 10 + NX * core + d],
            device_id={"blk": hop(d), "pipe": section}, device_id_type=MESH,
        )

    def reduce_siblings(section):
        for d in (1, 2, 3, 0):
            rows = aligned(lax.rem(coord2 + d, NX), PIECE)
            stage0[section, d] = grads[section, other, rows, :].astype(BF16)
            sib_copy(section, d).start()

    def reduce_first(section):
        for d in (1, 2, 3, 0):
            rows = aligned(lax.rem(coord1 + d, NX), PIECE)
            sib_copy(section, d).wait()
            value = grads[section, core, rows, :] + sib[section, d].astype(F32)
            if d:
                stage1[section, d] = value.astype(BF16)
            else:
                acc1[section] = value

    def first_piece(section, d, r):
        rows = aligned(r, 16)
        pltpu.make_async_remote_copy(
            src_ref=stage1.at[section, d, rows], dst_ref=land1.at[section, d, rows],
            send_sem=red_send.at[section, 4 + d], recv_sem=red_recv.at[section, 4 + d],
            device_id={"blk": hop(d)}, device_id_type=MESH,
        ).start()

    def first_spread(step):
        @pl.when((step >= 1) & (step <= 3 * (PIECE // 16)))
        def _():
            index = step - 1
            first_piece(1, 1 + lax.rem(index, 3), lax.div(index, 3))

    def first_burst(step):
        for d in range(1, NX):
            first_piece(0, d, step)

    def last_piece(section, d, u, rows):
        pltpu.make_async_remote_copy(
            src_ref=total.at[section, u, rows], dst_ref=gx.at[core, coord1, u, rows],
            send_sem=red_send.at[section, 10 + d], recv_sem=red_recv.at[section, 10 + NX * core + d],
            device_id={"blk": hop(d), "pipe": section}, device_id_type=MESH,
        ).start()

    def last_burst(part):
        def extra(step):
            index = step + part * GROUP
            rows = aligned(lax.rem(index, 2), SUB // 2)
            for d in range(1, NX):
                last_piece(1, d, lax.div(index, 2), rows)

        return extra

    def reduce_plane(section):
        for d in range(1, NX):
            first_copy(section, d).wait()
        value = acc1[section]
        for d in range(1, NX):
            value = value + land1[section, d].astype(F32)
        acc1[section] = value
        stage2[section] = value.astype(BF16).reshape(PLANE, SUB, T)

        def send(u, carry):
            c2, cz = plane(u)
            plane_copy(section, u, stage2.at[section, c2 * NZ + cz], land2.at[section, u - 1], 8).start()
            return carry

        lax.fori_loop(1, PLANE, send, 0)

    def gather_plane(section):
        mine = coord2 * NZ + pz
        await_plane(land2, section, 8)

        def add(u, value):
            return value + land2[section, u].astype(F32)

        value = lax.fori_loop(0, PLANE - 1, add, acc1[section, aligned(mine, SUB), :], unroll=True)
        total[section, mine] = value.astype(BF16)

        def send(u, carry):
            plane_copy(section, u, total.at[section, mine], total.at[section, mine], 9).start()
            return carry

        lax.fori_loop(1, PLANE, send, 0)

    def gather_last(section, pieces=False):
        await_plane(total, section, 9)
        if not pieces:
            for d in range(1, NX):
                last_copy(section, d).start()

        @pl.when(core == section)
        def _():
            pltpu.make_async_copy(
                total.at[section], gx.at[core, coord1], red_recv.at[section, 10 + NX * core]
            ).start()

        @pl.when(core != section)
        def _():
            last_copy(section, 0).start()

    def await_last():
        for h in range(2):
            for d in range(NX):
                part = gx.at[h, d]
                pltpu.make_async_copy(part, part, red_recv.at[core, 10 + NX * h + d]).wait()

    def await_last_sends():
        for section in range(2):
            for d in range(1, NX):
                last_copy(section, d).wait_send()

            @pl.when(core != section)
            def _():
                last_copy(section, 0).wait_send()

    def unpack(half, out):
        def step(b, carry):
            rows = aligned(lax.rem(b, 8), 4)
            block = gx[half, lax.div(b, 8), rows].reshape(NK, T)
            out[2 * b] = block[:, :NK]
            out[2 * b + 1] = block[:, NK:]
            return carry

        lax.fori_loop(0, NK // 2, step, 0, unroll=4)

    for i in range(5):
        await_input(core, i)
    expand(core)
    expand_right(core)
    build_pairs(core)
    cot_copy.wait()
    pl.semaphore_wait(barrier, NB + NX + NY - 2)
    for i in (1, 0, 2, 3, 4):
        exchange_copy(i).start()
    await_input(other, 1)
    expand(other)

    @pl.when(core == 0)
    def _():
        await_input(1, 0)

    gate(1, gy_buf, send_b.at[1], 0, HALF)
    all_to_all(send_b.at[1], recv_b.at[1], 0, 0, 0, HALF)

    for i in (2, 3, 4):
        await_input(other, i)
    expand_right(other)
    build_pairs(other)
    forward(1, send_f.at[1])
    PART = HALF // 2
    for p in range(2):
        all_to_all(send_f.at[1], recv_f.at[1], 1 + p, 1 + p, p * PART, PART)

    @pl.when(core == 1)
    def _():
        await_input(0, 0)

    forward(0, send_f.at[0])

    await_block(recv_b.at[1], a2a_recv, 0, 0, HALF)
    channel_back(1, recv_b.at[1], 0, 1)
    reduce_siblings(1)
    channel_out(1)
    reduce_first(1)
    right_back(1, recv_b.at[1])

    acc[...] = jnp.zeros_like(acc)
    for p in range(2):
        await_block(recv_f.at[1], a2a_recv, 1 + p, p * PART, PART)
        carry_out(1, recv_f.at[1], gy_buf, p * PART, PART)
        gate(0, gi_buf.at[1], send_b.at[0], p * PART, PART)
        all_to_all(
            send_b.at[0], recv_b.at[0], 3 + p, 3 + p, p * PART, PART,
            extra=first_spread if p == 0 else None,
        )
        send_input_grad(1, p * PART, PART)
    finish_left(1)

    groups = [(p, g) for p in range(2) for g in range(NB // GROUP)]

    def pump(n, extra=None):
        if n >= 2:
            p, g = groups[n - 2]
            await_block(send_f.at[0], a2a_send, 5 + n - 2, p * PART, PART, 2 * GROUP)
        if n < len(groups):
            p, g = groups[n]
            all_to_all(send_f.at[0], recv_f.at[0], 5 + p, 5 + n, p * PART, PART, g * GROUP, GROUP, extra)

    await_block(recv_b.at[0], a2a_recv, 3, 0, PART)
    channel_back(0, recv_b.at[0], 0, 2)
    reduce_plane(1)
    pump(0)
    pump(1)
    await_block(recv_b.at[0], a2a_recv, 4, PART, PART)
    channel_back(0, recv_b.at[0], 1, 2, lambda: pump(2))
    reduce_siblings(0)
    gather_plane(1)
    channel_out(0)
    reduce_first(0)
    pump(3, first_burst)
    right_back(0, recv_b.at[0])
    reduce_plane(0)
    gather_last(1, True)
    pump(4, last_burst(0))
    pump(5, last_burst(1))
    gather_plane(0)
    pump(6)
    pump(7)
    acc[...] = jnp.zeros_like(acc)
    await_block(recv_f.at[0], a2a_recv, 5, 0, PART)
    carry_out(0, recv_f.at[0], gi_buf.at[1], 0, PART)
    send_input_grad(0, 0, PART)
    gather_last(0)
    await_block(recv_f.at[0], a2a_recv, 6, PART, PART)
    carry_out(0, recv_f.at[0], gi_buf.at[1], PART, PART)
    send_input_grad(0, PART, PART)
    finish_left(0)
    lr_copy = pltpu.make_async_remote_copy(
        src_ref=lr.at[other], dst_ref=lr_sib, send_sem=lr_send, recv_sem=lr_recv,
        device_id=sibling, device_id_type=MESH,
    )
    lr_copy.start()
    await_last()
    unpack(0, first_out)
    unpack(1, second_out)
    lr_copy.wait()
    right_out[...] = lr[core, 0] + lr_sib[0]
    left_out[...] = lr[core, 1] + lr_sib[1]
    await_last_sends()

    for i in range(5):
        exchange_copy(i).wait_send()
    await_block(send_b.at[1], a2a_send, 0, 0, HALF)
    for p in range(2):
        await_block(send_f.at[1], a2a_send, 1 + p, p * PART, PART)
        await_block(send_b.at[0], a2a_send, 3 + p, p * PART, PART)
    pump(8)
    pump(9)
    pltpu.make_async_copy(gi_buf.at[0], gi_own, gi_loc).wait()
    pltpu.make_async_copy(gi_buf.at[0], gi_own, gi_send).wait()
    pltpu.make_async_copy(gi_buf.at[0], gi_own, gi_recv).wait()


def body(x_saved, cotangent, seq_right, seq_left, chan_first, chan_second):
    v, dma = pltpu.VMEM, pltpu.SemaphoreType.DMA
    anywhere = pl.BlockSpec(memory_space=pl.ANY)
    vmem = pl.BlockSpec(memory_space=pltpu.VMEM)
    own, theirs, right, left, first, second = pl.pallas_call(
        kernel,
        name="monarch_backward",
        out_shape=[
            jax.ShapeDtypeStruct((T, D), BF16),
            jax.ShapeDtypeStruct((T, D), BF16),
            jax.ShapeDtypeStruct((T, T), F32),
            jax.ShapeDtypeStruct((T, T), F32),
            jax.ShapeDtypeStruct((NK, NK, NK), BF16),
            jax.ShapeDtypeStruct((NK, NK, NK), BF16),
        ],
        in_specs=[anywhere] * 6,
        out_specs=[anywhere] * 2 + [vmem] * 4,
        scratch_shapes=[
            v((2, T, D), BF16), v((2, T, T), BF16), v((2, T, T), BF16),
            v((2, D, NK), BF16), v((2, NK, NK, NK), BF16),
            v((T, D), BF16), v((2, T, D), BF16), v((2 * T, HALF), BF16), v((2, D, T), BF16),
            v((NK, NK, T), BF16), v((3, NK, NK, T), BF16), v((2, HALF, 2 * T), BF16),
            v((HALF, 2 * T), BF16), v((T, D), F32),
            v((2, 2 * T, 2 * T), BF16), v((2, 2 * T, 2 * T), BF16), v((2, 2 * T, 2 * T), BF16),
            v((2, 2 * T, HALF), BF16), v((2, 2 * T, HALF), BF16),
            v((2, 2 * T, HALF), BF16), v((2, 2 * T, HALF), BF16),
            v((7, 2, HALF), BF16), v((2 * T, 2 * T), F32), v((2 * T, T), F32),
            v((2, 2, HR, T), F32), v((2, NX, HR // NX, T), BF16), v((2, NX, HR // NX, T), BF16),
            v((2, NX, HR // NX, T), BF16), v((2, NX, HR // NX, T), BF16), v((2, HR // NX, T), F32),
            v((2, NY * NZ, HR // NB, T), BF16), v((2, NY * NZ, HR // NB, T), BF16),
            v((2, NY * NZ, HR // NB, T), BF16), v((2, NX, NY * NZ, HR // NB, T), BF16),
            v((2, 2, T, T), F32), v((2, T, T), F32), v((T, T), F32),
            dma((2, 5)), dma((5,)), dma, dma((13,)), dma((7,)), dma((2, 18)), dma((2, 18)),
            dma, dma, dma, dma, dma,
        ],
        compiler_params=pltpu.CompilerParams(
            collective_id=1, has_side_effects=True, vmem_limit_bytes=64_000_000
        ),
    )(
        x_saved[0], cotangent, seq_right[0, 0], seq_left[0, 0],
        chan_first[0].reshape(D, NK), chan_second[0],
    )

    low = lax.axis_index("pipe") == 0
    gi = jnp.stack([jnp.where(low, own, theirs), jnp.where(low, theirs, own)])
    return (
        gi[None], right[None, None], left[None, None],
        first.astype(F32)[None], second.astype(F32)[None],
    )


def solution(mesh):
    in_specs = (
        P("pipe", None, "blk", None),
        P(None, "blk", None),
        P("pipe", "blk", None, None),
        P("pipe", "blk", None, None),
        P("pipe", None, None, None),
        P("pipe", None, None, None),
    )
    out_specs = (
        P("pipe", None, "blk", None),
        P("pipe", "blk", None, None),
        P("pipe", "blk", None, None),
        P("pipe", None, None, None),
        P("pipe", None, None, None),
    )
    return jax.shard_map(body, mesh=mesh, in_specs=in_specs, out_specs=out_specs, check_vma=False)
```

```python
import jax
import jax.numpy as jnp
from jax import lax
from jax.experimental import pallas as pl
from jax.experimental.pallas import tpu as pltpu
from jax.sharding import PartitionSpec as P

MESH = pl.DeviceIdType.MESH
F32, BF16 = jnp.float32, jnp.bfloat16
NX, NZ, NY = 4, 8, 4
NB = NX * NZ * NY
T = 128
D = 4096
HALF = D // 2
NK = 64
TILE = 512
HR = 2048


def mm(a, b, ca=1, cb=0):
    return lax.dot_general(a, b, (((ca,), (cb,)), ((), ())), preferred_element_type=F32)


def aligned(index, size):
    return pl.ds(pl.multiple_of(index * size, size), size)


def kernel(
    x_in, cot_in, right_in, left_in, first_in, second_in,
    gi_own, gi_sib, right_out, left_out, first_out, second_out,
    x_buf, right_buf, left_buf, first_buf, second_buf,
    gy_buf, gi_buf, gate_buf, pair_buf, mt_buf, mk_buf, ht_buf, hg_buf, cb_buf,
    rexp, lexp, lexp_t,
    send_f, recv_f, send_b, recv_b, dummy, acc, tmp,
    grads, stage0, sib, stage1, land1, acc1, stage2, land2, total, gx, lr, lr_sib, left_sum,
    in_sem, ex_sem, cot_sem, a2a_send, a2a_recv, red_send, red_recv,
    gi_loc, gi_send, gi_recv, lr_send, lr_recv,
):
    me = lax.axis_index("blk")
    core = lax.axis_index("pipe")
    other = 1 - core
    sibling = {"pipe": other}
    px, pz, py = lax.div(me, NZ * NY), lax.rem(lax.div(me, NY), NZ), lax.rem(me, NY)

    local = (
        (x_in.at[core], x_buf), (left_in, left_buf), (right_in, right_buf),
        (first_in, first_buf), (second_in, second_buf),
    )
    for i, (src, dst) in enumerate(local):
        pltpu.make_async_copy(src, dst.at[core], in_sem.at[core, i]).start()
    cot_copy = pltpu.make_async_copy(cot_in.at[core], gy_buf, cot_sem)
    cot_copy.start()

    barrier = pltpu.get_barrier_semaphore()

    def greet(step, carry):
        peer = lax.rem(me + step, NB)
        pl.semaphore_signal(barrier, inc=1, device_id={"blk": peer}, device_id_type=MESH)
        return carry

    pl.semaphore_signal(barrier, inc=1, device_id=sibling, device_id_type=MESH)
    lax.fori_loop(1, NB, greet, 0)
    for d in range(1, NX):
        for axis_peer in (
            me + (lax.rem(px + d, NX) - px) * (NZ * NY),
            me + (lax.rem(py + d, NY) - py),
        ):
            pl.semaphore_signal(
                barrier, inc=1, device_id={"blk": axis_peer, "pipe": other}, device_id_type=MESH
            )

    remote = (
        (x_in.at[other], x_buf), (left_in, left_buf), (right_in, right_buf),
        (first_in, first_buf), (second_in, second_buf),
    )

    def exchange_copy(i):
        src, dst = remote[i]
        return pltpu.make_async_remote_copy(
            src_ref=src, dst_ref=dst.at[core], send_sem=ex_sem.at[i], recv_sem=in_sem.at[core, i],
            device_id=sibling, device_id_type=MESH,
        )

    def await_input(section, i):
        ref = (x_buf, left_buf, right_buf, first_buf, second_buf)[i].at[section]
        pltpu.make_async_copy(ref, ref, in_sem.at[section, i]).wait()

    def all_to_all(src, dst, recv_id, send_id, lo, size, first=0, count=NB, extra=None):
        columns = pl.ds(lo, size)

        def rows(i):
            return pl.ds(pl.multiple_of(2 * i, 2), 2)

        def send(step, carry):
            peer = lax.rem(me + step, NB)
            pltpu.make_async_remote_copy(
                src_ref=src.at[rows(peer), columns], dst_ref=dst.at[rows(me), columns],
                send_sem=a2a_send.at[send_id], recv_sem=a2a_recv.at[recv_id],
                device_id={"blk": peer}, device_id_type=MESH,
            ).start()
            if extra is not None:
                extra(step - first)
            return carry

        lax.fori_loop(max(first, 1), first + count, send, 0)
        if first == 0:
            if extra is not None:
                extra(jnp.int32(0))
            pltpu.make_async_copy(
                src.at[rows(me), columns], dst.at[rows(me), columns], a2a_recv.at[recv_id]
            ).start()
            pltpu.make_async_copy(
                src.at[rows(me), columns], dummy.at[recv_id, :, columns], a2a_send.at[send_id]
            ).start()

    def await_block(ref, sem, ident, lo, size, rows=2 * T):
        part = ref.at[pl.ds(0, rows), pl.ds(lo, size)]
        pltpu.make_async_copy(part, part, sem.at[ident]).wait()

    def expand(section):
        row = lax.broadcasted_iota(jnp.int32, (2 * T, T), 0)
        col = lax.broadcasted_iota(jnp.int32, (2 * T, T), 1)
        left = left_buf[section]
        for h in range(2):
            spread = (row == 2 * col + h).astype(F32).astype(BF16)
            part = slice(h * T, (h + 1) * T)
            lexp[section, part, :] = mm(left, spread, 1, 1).astype(BF16)
            lexp_t[section, :, part] = mm(spread, left, 1, 1).astype(BF16)

    def expand_right(section):
        row = lax.broadcasted_iota(jnp.int32, (2 * T, T), 0)
        col = lax.broadcasted_iota(jnp.int32, (2 * T, T), 1)
        right = right_buf[section]
        for h in range(2):
            spread = (row == 2 * col + h).astype(F32).astype(BF16)
            part = slice(h * T, (h + 1) * T)
            rexp[section, :, part] = mm(spread, right).astype(BF16)

    def build_pairs(section):
        row = lax.broadcasted_iota(jnp.int32, (NK, T), 0)
        col = lax.broadcasted_iota(jnp.int32, (NK, T), 1)
        twice = ((col == row) | (col == row + NK)).astype(F32).astype(BF16)
        low = lax.broadcasted_iota(jnp.int32, (T, T), 0) < NK
        first_half = lax.broadcasted_iota(jnp.int32, (T, T), 1) < NK

        def step(b, carry):
            rows = aligned(b, T)
            both = mm(first_buf[section, rows, :], twice)
            pair_buf[section, rows, :] = jnp.where(low == first_half, both, 0.0).astype(BF16)
            return carry

        lax.fori_loop(0, NK // 2, step, 0, unroll=4)

    def gate(section, grad_out, sent, lo, size):
        def step(i, carry):
            off = lo + i * TILE
            cs = pl.ds(pl.multiple_of(off, TILE), TILE)
            for h in range(2):
                wide = pl.ds(pl.multiple_of(off + h * HALF, TILE), TILE)
                value = grad_out[:, wide].astype(F32) * x_buf[section, :, wide].astype(F32)
                gate_buf[h * T : (h + 1) * T, cs] = value.astype(BF16)
            sent[:, cs] = mm(lexp_t[section], gate_buf[:, cs]).astype(BF16)
            return carry

        lax.fori_loop(0, size // TILE, step, 0)

    def swap_blocks(src, dst, lo, size):
        ps = pl.ds(lo, size)

        def step(g, carry):
            qs = aligned(g, 16)
            dst[qs, ps, :] = jnp.swapaxes(src[ps, qs, :], 0, 1)
            return carry

        lax.fori_loop(0, NK // 16, step, 0)

    def forward(section, sent):
        def mixed(b, carry):
            cols = aligned(b, T)
            out = mm(pair_buf[section, cols, :], x_buf[section, :, cols], 1, 1)
            mt_buf[aligned(b, 2)] = out.astype(BF16).reshape(2, NK, T)
            return carry

        lax.fori_loop(0, NK // 2, mixed, 0, unroll=4)
        swap_blocks(mt_buf, mk_buf.at[section], 0, NK)

        def hidden(k, carry):
            rows = aligned(k, NK)
            for h in range(2):
                kk = k + h * (NK // 2)
                out = mm(second_buf[section, kk], mk_buf[section, kk])
                ht_buf[section, rows, h * T : (h + 1) * T] = out.astype(BF16)
            return carry

        lax.fori_loop(0, NK // 2, hidden, 0, unroll=4)

        def rows_of(i, carry):
            cs = aligned(i, TILE)
            sent[:, cs] = mm(rexp[section], ht_buf[section, cs, :], 1, 1).astype(BF16)
            return carry

        lax.fori_loop(0, HALF // TILE, rows_of, 0)

    def fold(target):
        even = lax.rem(lax.broadcasted_iota(jnp.int32, (2 * T, T), 0), 2) == 0
        tmp[...] = jnp.where(even, acc[:, :T], acc[:, T:])
        target[...] = tmp[pl.ds(0, T, stride=2), :] + tmp[pl.ds(1, T, stride=2), :]

    def right_back(section, returned):
        acc[...] = jnp.zeros_like(acc)

        def step(i, carry):
            cs = aligned(i, TILE)
            acc[...] += mm(returned[:, cs], ht_buf[section, cs, :])
            return carry

        lax.fori_loop(0, HALF // TILE, step, 0)
        fold(lr.at[section, 0])

    def channel_back(section, returned, lo, size, between=None):
        pairs = size // T
        first_half = lax.broadcasted_iota(jnp.int32, (NK, T), 1) < NK

        def step(i, carry):
            cs = aligned(i, TILE)
            hg_buf[cs, :] = mm(returned[:, cs], rexp[section], 0, 0).astype(BF16)
            return carry

        lax.fori_loop(lo // TILE, (lo + size) // TILE, step, 0)

        def pair(b, carry):
            for h in range(2):
                k0 = 2 * b + h * (NK // 2)
                grad = hg_buf[aligned(b, T), h * T : (h + 1) * T]
                mix = mk_buf[section, pl.ds(k0, 2)].reshape(T, T)
                outer = mm(grad, mix, 1, 1)
                grads[section, 1, pl.ds(pl.multiple_of(k0 * (NK // 2), NK), NK), :] = jnp.where(
                    first_half, outer[:NK], outer[NK:]
                )
                for q in range(2):
                    back = mm(second_buf[section, k0 + q], grad[q * NK : (q + 1) * NK], 0, 0)
                    mt_buf[k0 + q] = back.astype(BF16)
            return carry

        lax.fori_loop(lo // T, lo // T + pairs, pair, 0, unroll=2)
        for h in range(2):
            swap_blocks(mt_buf, mg_view, h * (NK // 2) + lo // NK, 2 * pairs)
        if between is None:
            return
        between()

        def columns(b, carry):
            cols = aligned(b, T)
            mixed_grad = mg_view[aligned(b, 2)].reshape(T, T)
            outer = mm(mixed_grad, x_buf[section, :, cols])
            grads[section, 0, aligned(b, NK), :] = jnp.where(first_half, outer[:NK], outer[NK:])
            return carry

        lax.fori_loop(0, NK // 2, columns, 0, unroll=4)

    def channel_out(section):
        def columns(b, carry):
            cols = aligned(b, T)
            mixed_grad = mg_view[aligned(b, 2)].reshape(T, T)
            cb_buf[:, cols] = mm(mixed_grad, pair_buf[section, cols, :], 0, 0)
            return carry

        lax.fori_loop(0, NK // 2, columns, 0, unroll=4)

    mg_view = mk_buf.at[2]

    def carry_out(section, gathered, grad_out, lo, size):
        def step(i, carry):
            off = lo + i * TILE
            cs = pl.ds(pl.multiple_of(off, TILE), TILE)
            block = gathered[:, cs]
            carried = mm(lexp[section], block)
            for h in range(2):
                wide = pl.ds(pl.multiple_of(off + h * HALF, TILE), TILE)
                value = grad_out[:, wide].astype(F32) * carried[h * T : (h + 1) * T] + cb_buf[:, wide]
                gi_buf[section, :, wide] = value.astype(BF16)
            acc[...] += mm(block, gate_buf[:, cs], 1, 1)
            return carry

        lax.fori_loop(0, size // TILE, step, 0)

    def finish_left(section):
        fold(left_sum)
        lr[section, 1] = left_sum[...].T

    def send_input_grad(section, lo, size):
        for h in range(2):
            cols = pl.ds(h * HALF + lo, size)
            src = gi_buf.at[section, :, cols]

            @pl.when(core == section)
            def _():
                pltpu.make_async_copy(src, gi_own.at[:, cols], gi_loc).start()

            @pl.when(core != section)
            def _():
                pltpu.make_async_remote_copy(
                    src_ref=src, dst_ref=gi_sib.at[:, cols], send_sem=gi_send, recv_sem=gi_recv,
                    device_id=sibling, device_id_type=MESH,
                ).start()

    is_low = core == 0
    coord1, coord2 = jnp.where(is_low, px, py), jnp.where(is_low, py, px)
    stride1, stride2 = jnp.where(is_low, NZ * NY, 1), jnp.where(is_low, 1, NZ * NY)
    GROUP = 32
    PIECE = HR // NX
    PLANE = NY * NZ
    SUB = PIECE // PLANE

    def hop(d):
        return me + (lax.rem(coord1 + d, NX) - coord1) * stride1

    def sib_copy(section, d):
        return pltpu.make_async_remote_copy(
            src_ref=stage0.at[section, d], dst_ref=sib.at[section, d],
            send_sem=red_send.at[section, d], recv_sem=red_recv.at[section, d],
            device_id=sibling, device_id_type=MESH,
        )

    def first_copy(section, d):
        return pltpu.make_async_remote_copy(
            src_ref=stage1.at[section, d], dst_ref=land1.at[section, d],
            send_sem=red_send.at[section, 4 + d], recv_sem=red_recv.at[section, 4 + d],
            device_id={"blk": hop(d)}, device_id_type=MESH,
        )

    def plane(u):
        return lax.rem(coord2 + lax.div(u, NZ), NY), lax.rem(pz + lax.rem(u, NZ), NZ)

    def plane_copy(section, u, src, dst, sem):
        c2, cz = plane(u)
        peer = me + (c2 - coord2) * stride2 + (cz - pz) * NY
        return pltpu.make_async_remote_copy(
            src_ref=src, dst_ref=dst, send_sem=red_send.at[section, sem], recv_sem=red_recv.at[section, sem],
            device_id={"blk": peer}, device_id_type=MESH,
        )

    def await_plane(ref, section, sem):
        part = ref.at[section, pl.ds(0, PLANE - 1)]
        pltpu.make_async_copy(part, part, red_send.at[section, sem]).wait()
        pltpu.make_async_copy(part, part, red_recv.at[section, sem]).wait()

    def last_copy(section, d):
        return pltpu.make_async_remote_copy(
            src_ref=total.at[section], dst_ref=gx.at[core, coord1],
            send_sem=red_send.at[section, 10 + d], recv_sem=red_recv.at[section, 10 + NX * core + d],
            device_id={"blk": hop(d), "pipe": section}, device_id_type=MESH,
        )

    def reduce_siblings(section):
        for d in (1, 2, 3, 0):
            rows = aligned(lax.rem(coord2 + d, NX), PIECE)
            stage0[section, d] = grads[section, other, rows, :].astype(BF16)
            sib_copy(section, d).start()

    def reduce_first(section):
        for d in (1, 2, 3, 0):
            rows = aligned(lax.rem(coord1 + d, NX), PIECE)
            sib_copy(section, d).wait()
            value = grads[section, core, rows, :] + sib[section, d].astype(F32)
            if d:
                stage1[section, d] = value.astype(BF16)
            else:
                acc1[section] = value

    def first_piece(section, d, r):
        rows = aligned(r, 16)
        pltpu.make_async_remote_copy(
            src_ref=stage1.at[section, d, rows], dst_ref=land1.at[section, d, rows],
            send_sem=red_send.at[section, 4 + d], recv_sem=red_recv.at[section, 4 + d],
            device_id={"blk": hop(d)}, device_id_type=MESH,
        ).start()

    def first_spread(step):
        @pl.when((step >= 1) & (step <= 3 * (PIECE // 16)))
        def _():
            index = step - 1
            first_piece(1, 1 + lax.rem(index, 3), lax.div(index, 3))

    def first_burst(step):
        for d in range(1, NX):
            first_piece(0, d, step)

    def last_piece(section, d, u, rows):
        pltpu.make_async_remote_copy(
            src_ref=total.at[section, u, rows], dst_ref=gx.at[core, coord1, u, rows],
            send_sem=red_send.at[section, 10 + d], recv_sem=red_recv.at[section, 10 + NX * core + d],
            device_id={"blk": hop(d), "pipe": section}, device_id_type=MESH,
        ).start()

    def last_burst(part):
        def extra(step):
            index = step + part * GROUP
            rows = aligned(lax.rem(index, 2), SUB // 2)
            for d in range(1, NX):
                last_piece(1, d, lax.div(index, 2), rows)

        return extra

    def reduce_plane(section):
        for d in range(1, NX):
            first_copy(section, d).wait()
        value = acc1[section]
        for d in range(1, NX):
            value = value + land1[section, d].astype(F32)
        acc1[section] = value
        stage2[section] = value.astype(BF16).reshape(PLANE, SUB, T)

        def send(u, carry):
            c2, cz = plane(u)
            plane_copy(section, u, stage2.at[section, c2 * NZ + cz], land2.at[section, u - 1], 8).start()
            return carry

        lax.fori_loop(1, PLANE, send, 0)

    def gather_plane(section):
        mine = coord2 * NZ + pz
        await_plane(land2, section, 8)

        def add(u, value):
            return value + land2[section, u].astype(F32)

        value = lax.fori_loop(0, PLANE - 1, add, acc1[section, aligned(mine, SUB), :], unroll=True)
        total[section, mine] = value.astype(BF16)

        def send(u, carry):
            plane_copy(section, u, total.at[section, mine], total.at[section, mine], 9).start()
            return carry

        lax.fori_loop(1, PLANE, send, 0)

    def gather_last(section, pieces=False):
        await_plane(total, section, 9)
        if not pieces:
            for d in range(1, NX):
                last_copy(section, d).start()

        @pl.when(core == section)
        def _():
            pltpu.make_async_copy(
                total.at[section], gx.at[core, coord1], red_recv.at[section, 10 + NX * core]
            ).start()

        @pl.when(core != section)
        def _():
            last_copy(section, 0).start()

    def await_last():
        for h in range(2):
            for d in range(NX):
                part = gx.at[h, d]
                pltpu.make_async_copy(part, part, red_recv.at[core, 10 + NX * h + d]).wait()

    def await_last_sends():
        for section in range(2):
            for d in range(1, NX):
                last_copy(section, d).wait_send()

            @pl.when(core != section)
            def _():
                last_copy(section, 0).wait_send()

    def unpack(half, out):
        def step(b, carry):
            rows = aligned(lax.rem(b, 8), 4)
            block = gx[half, lax.div(b, 8), rows].reshape(NK, T)
            out[2 * b] = block[:, :NK]
            out[2 * b + 1] = block[:, NK:]
            return carry

        lax.fori_loop(0, NK // 2, step, 0, unroll=4)

    for i in range(5):
        await_input(core, i)
    expand(core)
    expand_right(core)
    build_pairs(core)
    cot_copy.wait()
    pl.semaphore_wait(barrier, NB + NX + NY - 2)
    for i in (1, 0, 2, 3, 4):
        exchange_copy(i).start()
    await_input(other, 1)
    expand(other)

    @pl.when(core == 0)
    def _():
        await_input(1, 0)

    gate(1, gy_buf, send_b.at[1], 0, HALF)
    all_to_all(send_b.at[1], recv_b.at[1], 0, 0, 0, HALF)

    for i in (2, 3, 4):
        await_input(other, i)
    expand_right(other)
    build_pairs(other)
    forward(1, send_f.at[1])
    PART = HALF // 2
    CUT = 2 * TILE
    spans = ((0, CUT), (CUT, HALF - CUT))
    for p, (lo, size) in enumerate(spans):
        all_to_all(send_f.at[1], recv_f.at[1], 1 + p, 1 + p, lo, size)

    @pl.when(core == 1)
    def _():
        await_input(0, 0)

    forward(0, send_f.at[0])

    await_block(recv_b.at[1], a2a_recv, 0, 0, HALF)
    channel_back(1, recv_b.at[1], 0, HALF, lambda: None)
    reduce_siblings(1)
    channel_out(1)
    reduce_first(1)
    right_back(1, recv_b.at[1])

    acc[...] = jnp.zeros_like(acc)
    for p, (lo, size) in enumerate(spans):
        await_block(recv_f.at[1], a2a_recv, 1 + p, lo, size)
        carry_out(1, recv_f.at[1], gy_buf, lo, size)
        gate(0, gi_buf.at[1], send_b.at[0], lo, size)
        all_to_all(
            send_b.at[0], recv_b.at[0], 3 + p, 3 + p, lo, size,
            extra=first_spread if p == 0 else None,
        )
        send_input_grad(1, lo, size)
    finish_left(1)

    groups = [(p, g) for p in range(2) for g in range(NB // GROUP)]

    def pump(n, extra=None):
        if n >= 2:
            p, g = groups[n - 2]
            await_block(send_f.at[0], a2a_send, 5 + n - 2, p * PART, PART, 2 * GROUP)
        if n < len(groups):
            p, g = groups[n]
            all_to_all(send_f.at[0], recv_f.at[0], 5 + p, 5 + n, p * PART, PART, g * GROUP, GROUP, extra)

    await_block(recv_b.at[0], a2a_recv, 3, 0, CUT)
    channel_back(0, recv_b.at[0], 0, CUT)
    reduce_plane(1)
    pump(0)
    pump(1)
    await_block(recv_b.at[0], a2a_recv, 4, CUT, HALF - CUT)
    channel_back(0, recv_b.at[0], CUT, HALF - CUT, lambda: pump(2))
    reduce_siblings(0)
    gather_plane(1)
    reduce_first(0)
    pump(3, first_burst)
    channel_out(0)
    right_back(0, recv_b.at[0])
    reduce_plane(0)
    gather_last(1, True)
    pump(4)
    pump(5, last_burst(0))
    gather_plane(0)
    pump(6, last_burst(1))
    pump(7)
    acc[...] = jnp.zeros_like(acc)
    await_block(recv_f.at[0], a2a_recv, 5, 0, PART)
    carry_out(0, recv_f.at[0], gi_buf.at[1], 0, PART)
    send_input_grad(0, 0, PART)
    gather_last(0)
    await_block(recv_f.at[0], a2a_recv, 6, PART, PART)
    carry_out(0, recv_f.at[0], gi_buf.at[1], PART, PART)
    send_input_grad(0, PART, PART)
    finish_left(0)
    lr_copy = pltpu.make_async_remote_copy(
        src_ref=lr.at[other], dst_ref=lr_sib, send_sem=lr_send, recv_sem=lr_recv,
        device_id=sibling, device_id_type=MESH,
    )
    lr_copy.start()
    await_last()
    unpack(0, first_out)
    unpack(1, second_out)
    lr_copy.wait()
    right_out[...] = lr[core, 0] + lr_sib[0]
    left_out[...] = lr[core, 1] + lr_sib[1]
    await_last_sends()

    for i in range(5):
        exchange_copy(i).wait_send()
    await_block(send_b.at[1], a2a_send, 0, 0, HALF)
    for p, (lo, size) in enumerate(spans):
        await_block(send_f.at[1], a2a_send, 1 + p, lo, size)
        await_block(send_b.at[0], a2a_send, 3 + p, lo, size)
    pump(8)
    pump(9)
    pltpu.make_async_copy(gi_buf.at[0], gi_own, gi_loc).wait()
    pltpu.make_async_copy(gi_buf.at[0], gi_own, gi_send).wait()
    pltpu.make_async_copy(gi_buf.at[0], gi_own, gi_recv).wait()


def body(x_saved, cotangent, seq_right, seq_left, chan_first, chan_second):
    v, dma = pltpu.VMEM, pltpu.SemaphoreType.DMA
    anywhere = pl.BlockSpec(memory_space=pl.ANY)
    vmem = pl.BlockSpec(memory_space=pltpu.VMEM)
    own, theirs, right, left, first, second = pl.pallas_call(
        kernel,
        name="monarch_backward",
        out_shape=[
            jax.ShapeDtypeStruct((T, D), BF16),
            jax.ShapeDtypeStruct((T, D), BF16),
            jax.ShapeDtypeStruct((T, T), F32),
            jax.ShapeDtypeStruct((T, T), F32),
            jax.ShapeDtypeStruct((NK, NK, NK), BF16),
            jax.ShapeDtypeStruct((NK, NK, NK), BF16),
        ],
        in_specs=[anywhere] * 6,
        out_specs=[anywhere] * 2 + [vmem] * 4,
        scratch_shapes=[
            v((2, T, D), BF16), v((2, T, T), BF16), v((2, T, T), BF16),
            v((2, D, NK), BF16), v((2, NK, NK, NK), BF16),
            v((T, D), BF16), v((2, T, D), BF16), v((2 * T, HALF), BF16), v((2, D, T), BF16),
            v((NK, NK, T), BF16), v((3, NK, NK, T), BF16), v((2, HALF, 2 * T), BF16),
            v((HALF, 2 * T), BF16), v((T, D), F32),
            v((2, 2 * T, 2 * T), BF16), v((2, 2 * T, 2 * T), BF16), v((2, 2 * T, 2 * T), BF16),
            v((2, 2 * T, HALF), BF16), v((2, 2 * T, HALF), BF16),
            v((2, 2 * T, HALF), BF16), v((2, 2 * T, HALF), BF16),
            v((7, 2, HALF), BF16), v((2 * T, 2 * T), F32), v((2 * T, T), F32),
            v((2, 2, HR, T), F32), v((2, NX, HR // NX, T), BF16), v((2, NX, HR // NX, T), BF16),
            v((2, NX, HR // NX, T), BF16), v((2, NX, HR // NX, T), BF16), v((2, HR // NX, T), F32),
            v((2, NY * NZ, HR // NB, T), BF16), v((2, NY * NZ, HR // NB, T), BF16),
            v((2, NY * NZ, HR // NB, T), BF16), v((2, NX, NY * NZ, HR // NB, T), BF16),
            v((2, 2, T, T), F32), v((2, T, T), F32), v((T, T), F32),
            dma((2, 5)), dma((5,)), dma, dma((13,)), dma((7,)), dma((2, 18)), dma((2, 18)),
            dma, dma, dma, dma, dma,
        ],
        compiler_params=pltpu.CompilerParams(
            collective_id=1, has_side_effects=True, vmem_limit_bytes=64_000_000
        ),
    )(
        x_saved[0], cotangent, seq_right[0, 0], seq_left[0, 0],
        chan_first[0].reshape(D, NK), chan_second[0],
    )

    low = lax.axis_index("pipe") == 0
    gi = jnp.stack([jnp.where(low, own, theirs), jnp.where(low, theirs, own)])
    return (
        gi[None], right[None, None], left[None, None],
        first.astype(F32)[None], second.astype(F32)[None],
    )


def solution(mesh):
    in_specs = (
        P("pipe", None, "blk", None),
        P(None, "blk", None),
        P("pipe", "blk", None, None),
        P("pipe", "blk", None, None),
        P("pipe", None, None, None),
        P("pipe", None, None, None),
    )
    out_specs = (
        P("pipe", None, "blk", None),
        P("pipe", "blk", None, None),
        P("pipe", "blk", None, None),
        P("pipe", None, None, None),
        P("pipe", None, None, None),
    )
    return jax.shard_map(body, mesh=mesh, in_specs=in_specs, out_specs=out_specs, check_vma=False)
```
